512 devices in a mesh: gx: 8 (over x, core), gy: 8 (over z), gz: 8 (over y).
Axes of the slice: x: 4, y: 8, z: 8, core: 2. Of those that a mesh axis runs over, the one named last changes fastest.
Arguments:
- rhs: float32 [64, 128, 1024], P('gx', 'gy', 'gz'), may hold values from -5 to 5
- coef: float32 [64, 128, 1024], P('gx', 'gy', 'gz'), may hold values from 0.3 to 3
- agglom: int32 [512, 1], replicated, may hold values from 0 to 63, as said below
Outputs:
- solution: float32 [64, 128, 1024], P('gx', 'gy', 'gz')
The draws below stay inside these ranges and needn't reach their ends.
Inputs may be any that keep to these rules, and one draw needn't show every extreme that they name: `agglom`: every section device takes at least one block and at most 16; some takes exactly 16. The blocks of one section device are consecutive along the bit-alternated (Morton) order of the block grid, with the third dimension's bit lowest at each level.
All inputs are finite; a program needn't handle non-finite values.
Results may differ from the reference program's by a relative error of at most 0.0003.
Values sent between devices are 32-bit elements; how exact they have to be, the bound alone decides.
A program may use at most 64 MiB of HBM per device.

```python
import math
import jax
import jax.numpy as jnp
from jax import lax

CX = 8
CY = 16
CZ = 128
SLICE_LEVELS = 3
PRE = 2
POST = 2
CYCLES = 2
COARSE_SWEEPS = 8
MOST = 16
SECTION = 64
BLOCKS = 512
NX = 64
NY = 128
NZ = 1024
N_GX = 8
N_GY = 8
N_GZ = 8


def draw_rhs(key, part):
    grid_shape = (NX, NY, NZ)
    rough_part = jnp.clip(jax.random.normal(key, grid_shape, jnp.float32), -4.5, 4.5)
    height = 0.15
    along_x = jnp.sin(math.pi * (jnp.arange(NX, dtype=jnp.float32) + 0.5) / NX)
    along_y = jnp.sin(math.pi * (jnp.arange(NY, dtype=jnp.float32) + 0.5) / NY)
    along_z = jnp.sin(math.pi * (jnp.arange(NZ, dtype=jnp.float32) + 0.5) / NZ)
    smooth_part = along_x[:, None, None] * along_y[None, :, None] * along_z[None, None, :]
    return rough_part + height * smooth_part


def draw_agglom(key, part):
    numbers = jnp.arange(BLOCKS, dtype=jnp.int32)
    coord_x = numbers // (N_GY * N_GZ)
    coord_y = numbers // N_GZ % N_GY
    coord_z = numbers % N_GZ
    curve_key = jnp.zeros((BLOCKS,), jnp.int32)
    for level in range(6):
        place = 8 ** level
        step_size = 2 ** level
        curve_key = curve_key + coord_z // step_size % 2 * place
        curve_key = curve_key + coord_y // step_size % 2 * (2 * place)
        curve_key = curve_key + coord_x // step_size % 2 * (4 * place)
    curve_order = jnp.argsort(curve_key, stable=True).astype(jnp.int32)
    position = jnp.zeros((BLOCKS,), jnp.int32).at[curve_order].set(numbers)
    key_order = jax.random.fold_in(key, 11)
    key_big = jax.random.fold_in(key, 12)
    key_bias = jax.random.fold_in(key, 13)
    key_noise = jax.random.fold_in(key, 14)
    owner_order = jax.random.permutation(key_order, SECTION).astype(jnp.int32)
    big_run = jax.random.randint(key_big, (), 0, SECTION, dtype=jnp.int32)
    bias = jax.random.randint(key_bias, (SECTION,), 0, 4, dtype=jnp.int32)
    slot_count = SECTION * (MOST - 1)
    slot_numbers = jnp.arange(slot_count, dtype=jnp.int32)
    slot_run = slot_numbers // (MOST - 1)
    noise = jax.random.randint(key_noise, (slot_count,), 0, 1024, dtype=jnp.int32)
    scores = (bias[slot_run] * 512 + noise) * 2048 + slot_numbers
    scores = jnp.where(slot_run == big_run, -1, scores)
    extra_total = BLOCKS - MOST - SECTION + 1
    chosen = lax.top_k(scores, extra_total)[1]
    extras = jnp.zeros((SECTION,), jnp.int32).at[slot_run[chosen]].add(1)
    run_numbers = jnp.arange(SECTION, dtype=jnp.int32)
    lengths = jnp.where(run_numbers == big_run, MOST, 1 + extras).astype(jnp.int32)
    ends = jnp.cumsum(lengths).astype(jnp.int32)
    block_run_number = jnp.sum((ends[None, :] <= position[:, None]).astype(jnp.int32), axis=1)
    return owner_order[block_run_number].reshape(BLOCKS, 1).astype(jnp.int32)


def steps_of(own_key, extent, cuts, least, high):
    loudness, own = 1.0, jax.random.fold_in(own_key, 6)
    for dim, shards_of in cuts:
        heights = jnp.exp(jax.random.uniform(jax.random.fold_in(own, dim), (shards_of,), jnp.float32, least / len(cuts), high / len(cuts)))
        loudness = loudness * jnp.repeat(heights, extent[dim] // shards_of).reshape([-1 if axis == dim else 1 for axis in range(len(extent))])
    return loudness


def setup_inputs(seed: int = 0) -> dict:
    arg_keys = jax.random.split(jax.random.key(seed), 4)
    rhs = draw_rhs(jax.random.fold_in(arg_keys[3], 71), 0)
    coef = jnp.clip(jnp.exp(math.log(3.0) - 2.3025851 * jax.random.uniform(arg_keys[1], (NX, NY, NZ), jnp.float32) ** steps_of(arg_keys[1], (NX, NY, NZ), ((0, 8), (1, 8), (2, 8)), -0.2, 0.2)), 0.3, 3.0)
    agglom = draw_agglom(jax.random.fold_in(arg_keys[3], 71), 0)
    return {"rhs": rhs, "coef": coef, "agglom": agglom}


OMEGA = 0.8


def restrict(field):
    a, b, c = field.shape
    return field.reshape(a // 2, 2, b // 2, 2, c // 2, 2).mean(axis=(1, 3, 5))


def prolong(field):
    return jnp.repeat(jnp.repeat(jnp.repeat(field, 2, 0), 2, 1), 2, 2)


def shifted(padded):
    return (padded[2:, 1:-1, 1:-1], padded[:-2, 1:-1, 1:-1],
            padded[1:-1, 2:, 1:-1], padded[1:-1, :-2, 1:-1],
            padded[1:-1, 1:-1, 2:], padded[1:-1, 1:-1, :-2])


def face_weights(coeffs, padded):
    return tuple(0.5 * (coeffs + other) for other in shifted(padded))


def weighted(weights, others):
    total = weights[0] * others[0]
    for j in range(1, 6):
        total = total + weights[j] * others[j]
    return total


def diagonal_of(weights, factor):
    total = weights[0]
    for j in range(1, 6):
        total = total + weights[j]
    return factor * total


def reference(rhs, coef, agglom):
    levels = SLICE_LEVELS
    coeffs = [coef]
    for j in range(levels):
        coeffs.append(restrict(coeffs[-1]))
    weights = []
    diagonals = []
    for j in range(levels + 1):
        level_weights = face_weights(coeffs[j], jnp.pad(coeffs[j], 1))
        weights.append(level_weights)
        diagonals.append(diagonal_of(level_weights, 0.25 ** j))

    owner_grid = agglom[:, 0].reshape(N_GX, N_GY, N_GZ)
    span = 2 ** levels
    owner_cells = jnp.repeat(jnp.repeat(jnp.repeat(owner_grid, CX // span, 0), CY // span, 1), CZ // span, 2)
    owner_padded = jnp.pad(owner_cells, 1, constant_values=-1)
    masked = tuple(jnp.where(other == owner_cells, weight, 0.0)
                   for other, weight in zip(shifted(owner_padded), weights[levels]))
    coarse_factor = 0.25 ** levels

    def operate(values, level):
        return diagonals[level] * values - (0.25 ** level) * weighted(weights[level], shifted(jnp.pad(values, 1)))

    def smooth(values, source, level):
        return values + OMEGA * (source - operate(values, level)) / diagonals[level]

    def coarse_correct(source):
        diagonal = diagonals[levels]
        errors = OMEGA * source / diagonal
        for j in range(COARSE_SWEEPS - 1):
            coupled = weighted(masked, shifted(jnp.pad(errors, 1)))
            errors = errors + OMEGA * (source - (diagonal * errors - coarse_factor * coupled)) / diagonal
        return errors

    def vcycle(source, level):
        if level == levels:
            return coarse_correct(source)
        values = OMEGA * source / diagonals[level]
        for j in range(PRE - 1):
            values = smooth(values, source, level)
        residual = source - operate(values, level)
        values = values + prolong(vcycle(restrict(residual), level + 1))
        for j in range(POST):
            values = smooth(values, source, level)
        return values

    solution = jnp.zeros_like(rhs)
    for cycle in range(CYCLES):
        residual = rhs if cycle == 0 else rhs - operate(solution, 0)
        solution = solution + vcycle(residual, 0)
    return solution
```

```python
import jax
import jax.numpy as jnp
import numpy as np
from jax import lax
from jax.experimental import pallas as pl
from jax.experimental.pallas import tpu as pltpu
from jax.sharding import PartitionSpec as P

F32 = jnp.float32
BF16 = jnp.bfloat16
MESH = pl.DeviceIdType.MESH
OUT = -100000
COARSE_SWEEPS = 8
DIRS = [(dx, dy) for dx in (-1, 0, 1) for dy in (-1, 0, 1) if (dx, dy) != (0, 0)]
FAR = [(dx, dy) for dx in (-2, 2) for dy in (-1, 0, 1)]
XE0, YE0, H0 = 16, 24, 4
XE1, YE1, H1 = 14, 18, 5
L0, L1 = 384, 256
R0, R1, R2, R3 = 144, 80, 96, 48


def up128(n):
    return -(-n // 128) * 128


def lane0(x, y):
    return (y + H0) * XE0 + x + H0


def lane1(x, y):
    return (y + H1) * XE1 + x + H1


def tables(nx, ny):
    x2, y2 = 2 * nx, 4 * ny
    l2, l3 = up128(x2 * y2), up128(nx * 2 * ny)
    t = {}
    place0 = np.zeros((512, L0), np.float32)
    sel0 = np.zeros((32, L0), np.float32)
    unsel = np.zeros((128, L0), np.float32)
    for x in range(8):
        for y in range(16):
            place0[x * 16 + y, lane0(x, y)] = 1
            unsel[x * 16 + y, lane0(x, y)] = 1
            sel0[(x // 2) * 8 + y // 2, lane0(x, y)] = 0.125
    for s in range(2):
        for xi in range(4):
            for y in range(16):
                place0[128 + s * 64 + xi * 16 + y, lane0(xi - 4 if s == 0 else 8 + xi, y)] = 1
        for x in range(8):
            for yi in range(8):
                yy = yi - 8 if s == 0 else 16 + yi
                if -H0 <= yy < 16 + H0:
                    place0[256 + s * 64 + x * 8 + yi, lane0(x, yy)] = 1
        for q in range(2):
            for xi in range(4):
                for yi in range(8):
                    yy = yi - 8 if q == 0 else 16 + yi
                    if -H0 <= yy < 16 + H0:
                        place0[384 + (s * 2 + q) * 32 + xi * 8 + yi, lane0(xi - 4 if s == 0 else 8 + xi, yy)] = 1
    place1 = np.zeros((384, L1), np.float32)
    for d, (sx, sy) in enumerate([(0, 0)] + DIRS):
        for x in range(4):
            for y in range(8):
                xx, yy = x + 4 * sx, y + 8 * sy
                if -H1 <= xx < 4 + H1 and -H1 <= yy < 8 + H1:
                    place1[32 * d + x * 8 + y, lane1(xx, yy)] = 1
    for e, (sx, sy) in enumerate(FAR):
        for y in range(8):
            xx, yy = (-5 if sx < 0 else 8), y + 8 * sy
            if -H1 <= yy < 8 + H1:
                place1[288 + 8 * e + y, lane1(xx, yy)] = 1
    sel1 = np.zeros((8, L1), np.float32)
    for x in range(4):
        for y in range(8):
            sel1[(x // 2) * 4 + y // 2, lane1(x, y)] = 0.125
    prol0 = np.zeros((L1, L0), np.float32)
    for x in range(-H0, 8 + H0):
        for y in range(-H0, 16 + H0):
            prol0[lane1(x // 2, y // 2), lane0(x, y)] = 1
    perm2 = np.zeros((nx * ny * 8, l2), np.float32)
    for a in range(nx):
        for b in range(ny):
            for i in range(2):
                for j in range(4):
                    perm2[(a * ny + b) * 8 + i * 4 + j, (b * 4 + j) * x2 + a * 2 + i] = 1
    rest2 = np.zeros((l2, l3), np.float32)
    own3 = np.zeros((128, l3), np.float32)
    for x in range(x2):
        for y in range(y2):
            rest2[y * x2 + x, (y // 2) * nx + x // 2] = 0.125
    for x in range(nx):
        for y in range(2 * ny):
            own3[x * ny + y // 2, y * nx + x] = 1
    prol2 = (rest2.T != 0).astype(np.float32)
    kx1 = np.zeros((32, 128), np.float32)
    kx2 = np.zeros((8, 128), np.float32)
    for x in range(8):
        for y in range(16):
            kx1[(x // 2) * 8 + y // 2, x * 16 + y] = 0.25
            kx2[(x // 4) * 4 + y // 4, x * 16 + y] = 0.0625
    kz1 = np.zeros((128, 128), np.float32)
    kz2 = np.zeros((128, 128), np.float32)
    for z in range(128):
        kz1[z, z // 2] = 0.5
        for c in range(3):
            kz2[z, 32 * c + z // 4] = 0.25
    coord = np.full((16, max(L0, l2)), OUT, np.int32)
    for x in range(-H0, 8 + H0):
        for y in range(-H0, 16 + H0):
            coord[0:2, lane0(x, y)] = x, y
    for x in range(-H1, 4 + H1):
        for y in range(-H1, 8 + H1):
            coord[2:4, lane1(x, y)] = x, y
            coord[8, lane1(x, y)] = (y // 2) * x2 + x // 2
    for x in range(x2):
        for y in range(y2):
            coord[4:6, y * x2 + x] = x, y
    for x in range(nx):
        for y in range(2 * ny):
            coord[6:8, y * nx + x] = x, y
    names = dict(place0=place0, sel0=sel0, unsel=unsel, place1=place1, sel1=sel1, prol0=prol0, perm2=perm2, rest2=rest2,
                 own3=own3, prol2=prol2, kx1=kx1, kx2=kx2, kz1=kz1, kz2=kz2)
    t = {k: v.astype(jnp.bfloat16) for k, v in names.items()}
    t["coord"] = coord
    return t


def split(x):
    hi = x.astype(BF16)
    return hi, (x - hi.astype(F32)).astype(BF16)


def times(x, w):
    rows = x.shape[0]
    both = jnp.dot(jnp.concatenate(split(x), axis=0), w, preferred_element_type=F32)
    return both[:rows] + both[rows:]


def select_t(w, x):
    dims = (((1,), (1,)), ((), ()))
    hi, lo = split(x)
    return lax.dot_general(w, hi, dims, preferred_element_type=F32) + lax.dot_general(w, lo, dims, preferred_element_type=F32)


def left(w, x):
    hi, lo = split(x)
    return jnp.dot(w, hi, preferred_element_type=F32) + jnp.dot(w, lo, preferred_element_type=F32)


def build(nx, ny, nz):
    x2, y2 = 2 * nx, 4 * ny
    l2, l3 = up128(x2 * y2), up128(nx * 2 * ny)
    consts = tables(nx, ny)
    names = list(consts)

    n_sem = 3 * 10 + 3 * 16 + 3 * (2 + nx + ny)

    scratch = dict(
        xs0=pltpu.VMEM((3, 2, 4, 16, 128), F32),
        ys0=pltpu.VMEM((3, 2, 8, 8, 128), F32),
        ds0=pltpu.VMEM((3, 4, 4, 8, 128), F32),
        ext0=pltpu.VMEM((3, R0, L0), F32),
        nat1=pltpu.VMEM((3, 48, 8, 128), F32),
        ext1=pltpu.VMEM((3, R1, L1), F32),
        own2=pltpu.VMEM((3, 8, 128), F32),
        zs2=pltpu.VMEM((3, 2, 8, 128), F32),
        ys2=pltpu.VMEM((3, ny, 8, 128), F32),
        xs2=pltpu.VMEM((3, nx, ny, 8, 128), F32),
        sol=pltpu.VMEM((8, 16, 128), F32),
        m0=pltpu.VMEM((6, R0, L0), F32),
        c0=pltpu.VMEM((4, R0, L0), F32),
        m1=pltpu.VMEM((6, R1, L1), F32),
        c1=pltpu.VMEM((4, R1, L1), F32),
        m2=pltpu.VMEM((6, R2, l2), F32),
        c2=pltpu.VMEM((4, R2, l2), F32),
        m3=pltpu.VMEM((6, R3, l3), F32),
        c3=pltpu.VMEM((2, R3, l3), F32),
        pairs=pltpu.VMEM((max(L0, l2) // 128, 160, 128), F32),
        prol1=pltpu.VMEM((l2, L1), BF16),
        owners=pltpu.VMEM((8, l3), F32),
        ssem=pltpu.SemaphoreType.DMA((n_sem,)),
        rsem=pltpu.SemaphoreType.DMA((n_sem,)),
    )
    keys = list(scratch)

    def kernel(rhs, coef, agg, *rest):
        c = dict(zip(names, rest[: len(names)]))
        out = rest[len(names)]
        s = dict(zip(keys, rest[len(names) + 1:]))
        gx, gy, gz = lax.axis_index("gx"), lax.axis_index("gy"), lax.axis_index("gz")

        def has(dx, dy, dz):
            ok = None
            for g, d, n in ((gx, dx, nx), (gy, dy, ny), (gz, dz, nz)):
                if d:
                    here = (g + d >= 0) if d < 0 else (g + d < n)
                    ok = here if ok is None else ok & here
            return ok

        counter = [0]
        unsent = []

        class Copy:
            def __init__(self, src, dst, there, send_if, recv_if):
                i = counter[0]
                counter[0] += 1
                self.make = lambda: pltpu.make_async_remote_copy(
                    src_ref=src, dst_ref=dst, send_sem=s["ssem"].at[i], recv_sem=s["rsem"].at[i],
                    device_id=there, device_id_type=MESH)
                self.send_if, self.recv_if = send_if, recv_if
                unsent.append(self)

            def under(self, cond, f):
                if cond is None:
                    f()
                else:
                    pl.when(cond)(f)

            def start(self):
                self.under(self.send_if, lambda: self.make().start())

            def arrive(self):
                self.under(self.recv_if, lambda: self.make().wait_recv())

            def sent(self):
                self.under(self.send_if, lambda: self.make().wait_send())

        def toward(dx, dy, dz, src, dst):
            return Copy(src, dst, (gx + dx, gy + dy, gz + dz), has(dx, dy, dz), has(-dx, -dy, -dz))

        def plane0(n, src):
            copies = []
            for dx, dy in DIRS:
                xs = slice(0, 8) if dx == 0 else (slice(4, 8) if dx > 0 else slice(0, 4))
                ys = slice(0, 16) if dy == 0 else (slice(8, 16) if dy > 0 else slice(0, 8))
                a, b = (0 if dx > 0 else 1), (0 if dy > 0 else 1)
                if dy == 0:
                    dst = s["xs0"].at[n, a]
                elif dx == 0:
                    dst = s["ys0"].at[n, b]
                else:
                    dst = s["ds0"].at[n, 2 * a + b]
                copies.append(toward(dx, dy, 0, src.at[xs, ys, :], dst))
            return copies

        def z_halo(ref, n, rows):
            return [toward(0, 0, -1, ref.at[n, 8:16, :], ref.at[n, rows - 8:rows, :]),
                    toward(0, 0, 1, ref.at[n, rows - 16:rows - 8, :], ref.at[n, 0:8, :])]

        def plane1(n, far):
            copies = []
            for dx, dy in DIRS:
                d = 1 + DIRS.index((-dx, -dy))
                copies.append(toward(dx, dy, 0, s["nat1"].at[n, 0:4], s["nat1"].at[n, 4 * d:4 * d + 4]))
            if far:
                for dx, dy in FAR:
                    e = FAR.index((-dx, -dy))
                    i = 3 if dx > 0 else 0
                    copies.append(toward(dx, dy, 0, s["nat1"].at[n, i:i + 1], s["nat1"].at[n, 36 + e:37 + e]))
            return copies

        def z2(n):
            return [toward(0, 0, -1, s["own2"].at[n], s["zs2"].at[n, 1]),
                    toward(0, 0, 1, s["own2"].at[n], s["zs2"].at[n, 0])]

        def y2line(n):
            return [Copy(s["ys2"].at[n, gy], s["ys2"].at[n, gy], (gx, lax.rem(gy + d, ny), gz), None, None)
                    for d in range(1, ny)]

        def x2line(n):
            return [Copy(s["ys2"].at[n], s["xs2"].at[n, gx], (lax.rem(gx + d, nx), gy, gz), None, None)
                    for d in range(1, nx)]

        def start(copies):
            for copy in copies:
                copy.start()

        def arrive(copies):
            for copy in copies:
                copy.arrive()

        srcs = (rhs, coef, s["sol"])
        P0 = [plane0(n, srcs[n]) for n in range(3)]
        Z0 = [z_halo(s["ext0"], n, R0) for n in range(3)]
        P1 = [plane1(n, n == 0) for n in range(3)]
        Z1 = [z_halo(s["ext1"], n, R1) for n in range(3)]
        Z2 = [z2(n) for n in range(3)]
        Y2 = [y2line(n) for n in range(3)]
        X2 = [x2line(n) for n in range(3)]

        def clear(dx, dy, dz, dsts):
            @pl.when(jnp.logical_not(has(dx, dy, dz)))
            def _():
                for ref, index in dsts:
                    ref[index] = jnp.zeros(ref.at[index].shape, F32)

        for dx, dy in DIRS:
            a, b = (0 if dx < 0 else 1), (0 if dy < 0 else 1)
            d = 1 + DIRS.index((dx, dy))
            dsts = []
            for n in range(3):
                if dy == 0:
                    dsts.append((s["xs0"], (n, a)))
                elif dx == 0:
                    dsts.append((s["ys0"], (n, b)))
                else:
                    dsts.append((s["ds0"], (n, 2 * a + b)))
                dsts.append((s["nat1"], (n, slice(4 * d, 4 * d + 4))))
            clear(dx, dy, 0, dsts)
        for e, (dx, dy) in enumerate(FAR):
            clear(dx, dy, 0, [(s["nat1"], (0, slice(36 + e, 37 + e)))])
        for dz in (-1, 1):
            dsts = []
            for n in range(3):
                dsts.append((s["ext0"], (n, slice(0, 8) if dz < 0 else slice(R0 - 8, R0))))
                dsts.append((s["ext1"], (n, slice(0, 8) if dz < 0 else slice(R1 - 8, R1))))
                dsts.append((s["zs2"], (n, 0 if dz < 0 else 1)))
            clear(0, 0, dz, dsts)
        s["nat1"][0, 42:48] = jnp.zeros((6, 8, 128), F32)
        for n in (1, 2):
            s["nat1"][n, 36:48] = jnp.zeros((12, 8, 128), F32)

        barrier = pltpu.get_barrier_semaphore()
        total = jnp.int32(nx - 1 + ny - 1)
        for d in range(1, nx):
            pl.semaphore_signal(barrier, inc=1, device_id=(lax.rem(gx + d, nx), gy, gz), device_id_type=MESH)
        for d in range(1, ny):
            pl.semaphore_signal(barrier, inc=1, device_id=(gx, lax.rem(gy + d, ny), gz), device_id_type=MESH)
        near = [(dx, dy, 0) for dx, dy in DIRS + FAR if dx and dy] + [(0, 0, -1), (0, 0, 1)]
        for dx, dy, dz in near:
            ok = has(dx, dy, dz)
            total = total + ok.astype(jnp.int32)

            @pl.when(ok)
            def _(dx=dx, dy=dy, dz=dz):
                pl.semaphore_signal(barrier, inc=1, device_id=(gx + dx, gy + dy, gz + dz), device_id_type=MESH)
        pl.semaphore_wait(barrier, total)

        start(P0[1])
        start(P0[0])

        k_nat = coef[...].reshape(128, 128)
        k1 = times(left(c["kx1"][...], k_nat), c["kz1"][...])
        s["nat1"][0, 0:4] = k1.reshape(4, 8, 128)
        start(P1[0])
        k2_half = left(c["kx2"][...], k_nat)
        k2_half = jnp.concatenate([k2_half, k2_half], axis=0)
        s["own2"][0] = times(k2_half, c["kz2"][...])[0:8]
        start(Z2[0])

        def shifts(v, xe):
            rows, lanes = v.shape
            return (pltpu.roll(v, lanes - 1, 1), pltpu.roll(v, 1, 1), pltpu.roll(v, lanes - xe, 1), pltpu.roll(v, xe, 1),
                    pltpu.roll(v, rows - 1, 0), pltpu.roll(v, 1, 0))

        def setup(k, xe, factor, inside, inner, extra, m, consts_ref):
            rows, lanes = k.shape
            ws = []
            for i, other in enumerate(shifts(k, xe)):
                if inner is not None and i < 4:
                    other = jnp.where(inner[i], other, 0.0)
                ws.append(0.5 * (k + other))
            diag = ws[0]
            for w in ws[1:]:
                diag = diag + w
            diag = factor * diag
            minv = jnp.where(inside, 0.8 / diag, 0.0)
            for i, w in enumerate(ws):
                link = (factor * minv) * w
                if inner is not None and i < 4:
                    link = jnp.where(inner[i], link, 0.0)
                if extra is not None:
                    link = jnp.where(extra[i], link, 0.0)
                m[i] = link
            consts_ref[0] = minv
            if consts_ref.shape[0] > 2:
                consts_ref[1] = 1.25 * diag

        def sweep(v, g, m, xe):
            total = 0.2 * v + g
            for i, other in enumerate(shifts(v, xe)):
                total = total + m[i] * other
            return total

        def coords(level, lanes, rows, x_off, y_off, z_off):
            x = c["coord"][2 * level:2 * level + 1, 0:lanes] + x_off
            y = c["coord"][2 * level + 1:2 * level + 2, 0:lanes] + y_off
            z = lax.broadcasted_iota(jnp.int32, (rows, lanes), 0) + z_off
            return x, y, z

        def inside_of(x, y, z, sizes):
            plane = (x >= 0) & (x < sizes[0]) & (y >= 0) & (y < sizes[1])
            return jnp.broadcast_to(plane, z.shape) & (z >= 0) & (z < sizes[2])

        def assemble0(n, own):
            blocks = [own, s["xs0"][n].reshape(128, 128), s["ys0"][n].reshape(128, 128), s["ds0"][n].reshape(128, 128)]
            wide = jnp.concatenate([b.T for b in blocks], axis=1)
            s["ext0"][n, 8:R0 - 8] = times(wide, c["place0"][...])

        def assemble1(n):
            nat = s["nat1"][n].reshape(384, 128)
            wide = jnp.concatenate([nat[128 * i:128 * i + 128].T for i in range(3)], axis=1)
            s["ext1"][n, 8:R1 - 8] = times(wide[0:64], c["place1"][...])

        def gather2_y(n):
            arrive(Z2[n])
            lane = lax.broadcasted_iota(jnp.int32, (8, 128), 1)
            both = jnp.where(lane < 32, s["zs2"][n, 0], jnp.where(lane < 64, s["own2"][n], s["zs2"][n, 1]))
            s["ys2"][n, gy] = both
            start(Y2[n])

        def gather2_x(n):
            arrive(Y2[n])
            start(X2[n])
            s["xs2"][n, gx] = s["ys2"][n]

        def gather2(n):
            arrive(X2[n])
            nat = s["xs2"][n].reshape(nx * ny * 8, 128)
            step = min(128, nat.shape[0])
            wide = jnp.concatenate([nat[i:i + step].T for i in range(0, nat.shape[0], step)], axis=1)
            return times(wide[0:R2], c["perm2"][...])

        arrive(P0[1])
        assemble0(1, k_nat)
        start(Z0[1])
        arrive(P0[0])
        assemble0(0, rhs[...].reshape(128, 128))
        start(Z0[0])
        gather2_y(0)
        arrive(P1[0])
        assemble1(0)
        start(Z1[0])

        x1, y1, z1 = coords(1, L1, R1, 4 * gx, 8 * gy, 64 * gz - 8)
        target = c["coord"][8:9, 0:L1] + (2 * gx + 4 * gy * x2)
        target = jnp.where((x1 >= 0) & (x1 < 4 * nx) & (y1 >= 0) & (y1 < 8 * ny), target, -1)
        s["prol1"][...] = jnp.where(lax.broadcasted_iota(jnp.int32, (l2, L1), 0) == target, 1.0, 0.0).astype(BF16)

        s["owners"][...] = jnp.dot(agg[...].astype(BF16), c["own3"][...], preferred_element_type=F32)

        arrive(Z0[1])
        x0, y0, z0 = coords(0, L0, R0, 8 * gx, 16 * gy, 128 * gz - 8)
        setup(s["ext0"][1], XE0, 1.0, inside_of(x0, y0, z0, (8 * nx, 16 * ny, 128 * nz)), None, None, s["m0"], s["c0"])
        arrive(Z0[0])
        s["c0"][2] = s["c0"][0] * s["ext0"][0]

        def halved(v, first, half):
            rows, lanes = v.shape
            sums = []
            for j in range(lanes // 128):
                s["pairs"][j, 0:rows] = v[:, 128 * j:128 * j + 128]
                sums.append(s["pairs"][j, pl.ds(first, half, stride=2), :] + s["pairs"][j, pl.ds(first + 1, half, stride=2), :])
            return sums[0] if len(sums) == 1 else jnp.concatenate(sums, axis=1)

        def doubled(v, first, rows):
            half, lanes = v.shape
            parts = []
            for j in range(lanes // 128):
                part = v[:, 128 * j:128 * j + 128]
                s["pairs"][j, pl.ds(0, half, stride=2), :] = part
                s["pairs"][j, pl.ds(1, half, stride=2), :] = part
                parts.append(s["pairs"][j, first:first + rows])
            return parts[0] if len(parts) == 1 else jnp.concatenate(parts, axis=1)

        def down(m, consts_ref, xe):
            g = consts_ref[2]
            v = sweep(g, g, m, xe)
            consts_ref[3] = v
            return v

        def residual(v, g, m, consts_ref, xe):
            return consts_ref[1] * (sweep(v, g, m, xe) - v)

        for cycle in range(2):
            n = 1 + cycle
            v = down(s["m0"], s["c0"], XE0)
            r = residual(v, s["c0"][2], s["m0"], s["c0"], XE0)
            s["nat1"][n, 0:4, :, 0:64] = select_t(c["sel0"][...], halved(r, 8, 64)).reshape(4, 8, 64)
            start(P1[n])
            if cycle == 0:
                gather2_x(0)
                arrive(Z1[0])
                inside = inside_of(x1, y1, z1, (4 * nx, 8 * ny, 64 * nz))
                setup(s["ext1"][0], XE1, 0.25, inside, None, None, s["m1"], s["c1"])
            arrive(P1[n])
            assemble1(n)
            start(Z1[n])
            arrive(Z1[n])
            s["c1"][2] = s["c1"][0] * s["ext1"][n]
            v = down(s["m1"], s["c1"], XE1)
            half = halved(residual(v, s["c1"][2], s["m1"], s["c1"], XE1), 8, 32)
            s["own2"][n, :, 0:96] = select_t(c["sel1"][...], jnp.concatenate([half, half, half], axis=0))
            start(Z2[n])
            if cycle == 0:
                k2 = gather2(0)
                x, y, z = coords(2, l2, R2, 0, 0, 32 * gz - 32)
                inner = [jnp.broadcast_to(q, z.shape) for q in (x + 1 < x2, x > 0, y + 1 < y2, y > 0)]
                setup(k2, x2, 0.0625, inside_of(x, y, z, (x2, y2, 32 * nz)), inner, None, s["m2"], s["c2"])
                k3 = times(halved(k2, 0, R3), c["rest2"][...])
                x, y, z = coords(3, l3, R3, 0, 0, 16 * gz - 16)
                inner = [jnp.broadcast_to(q, z.shape) for q in (x + 1 < nx, x > 0, y + 1 < 2 * ny, y > 0)]
                low, high = jnp.maximum(gz - 1, 0), jnp.minimum(gz + 1, nz - 1)
                owner = jnp.concatenate([jnp.broadcast_to(s["owners"][pl.ds(i, 1), :], (16, l3)) for i in (low, gz, high)], axis=0)
                same = [other == owner for other in shifts(owner, nx)]
                setup(k3, nx, 0.015625, inside_of(x, y, z, (nx, 2 * ny, 16 * nz)), inner, same, s["m3"], s["c3"])
            gather2_y(n)
            gather2_x(n)
            f2 = gather2(n)
            s["c2"][2] = s["c2"][0] * f2
            v2 = down(s["m2"], s["c2"], x2)
            r = residual(v2, s["c2"][2], s["m2"], s["c2"], x2)
            g3 = s["c3"][0] * times(halved(r, 0, R3), c["rest2"][...])
            e = g3
            for j in range(COARSE_SWEEPS - 1):
                e = sweep(e, g3, s["m3"], nx)
            fine = times(e, c["prol2"][...])
            v = s["c2"][3] + doubled(fine, 0, R2)
            for j in range(2):
                v = sweep(v, s["c2"][2], s["m2"], x2)
            fine = times(v[24:72], s["prol1"][...])
            v = s["c1"][3] + doubled(fine, 8, R1)
            for j in range(2):
                v = sweep(v, s["c1"][2], s["m1"], XE1)
            fine = times(v, c["prol0"][...])
            v = s["c0"][3] + doubled(fine, 8, R0)
            for j in range(2):
                v = sweep(v, s["c0"][2], s["m0"], XE0)
            nat = select_t(c["unsel"][...], v[8:R0 - 8])
            if cycle == 0:
                s["sol"][...] = nat.reshape(8, 16, 128)
                start(P0[2])
                arrive(P0[2])
                assemble0(2, nat)
                start(Z0[2])
                arrive(Z0[2])
                now = s["ext0"][2]
                s["c0"][2] = sweep(now, s["c0"][0] * s["ext0"][0], s["m0"], XE0) - now
            else:
                out[...] = s["sol"][...] + nat.reshape(8, 16, 128)
        for copy in unsent:
            copy.sent()

    vmem = pl.BlockSpec(memory_space=pltpu.VMEM)

    def body(rhs, coef, agglom):
        agg = jnp.zeros((8, 128), F32).at[:nz, :nx * ny].set(agglom.reshape(nx * ny, nz).T.astype(F32))
        return pl.pallas_call(
            kernel,
            out_shape=jax.ShapeDtypeStruct((8, 16, 128), F32),
            in_specs=[vmem] * (3 + len(names)),
            out_specs=vmem,
            scratch_shapes=[scratch[k] for k in keys],
            compiler_params=pltpu.CompilerParams(collective_id=0, has_side_effects=True, vmem_limit_bytes=60 * 1024 * 1024),
        )(rhs, coef, agg, *[jnp.asarray(consts[k]) for k in names])

    return body


def solution(mesh):
    body = build(mesh.shape["gx"], mesh.shape["gy"], mesh.shape["gz"])
    spec = P("gx", "gy", "gz")
    return jax.shard_map(body, mesh=mesh, in_specs=(spec, spec, P()), out_specs=spec, check_vma=False)
```

```python
import jax
import jax.numpy as jnp
import numpy as np
from jax import lax
from jax.experimental import pallas as pl
from jax.experimental.pallas import tpu as pltpu
from jax.sharding import PartitionSpec as P

F32 = jnp.float32
BF16 = jnp.bfloat16
MESH = pl.DeviceIdType.MESH
OUT = -100000
COARSE_SWEEPS = 8
DIRS = [(dx, dy) for dx in (-1, 0, 1) for dy in (-1, 0, 1) if (dx, dy) != (0, 0)]
ALL = [(0, 0)] + DIRS
FAR = [(dx, dy) for dx in (-2, 2) for dy in (-1, 0, 1)]
XE0, YE0, H0 = 16, 24, 4
XE1, YE1, H1 = 14, 18, 5
L0, L1 = 384, 256
R0, R1, R2, R3 = 144, 80, 96, 48


def up128(n):
    return -(-n // 128) * 128


def lane0(x, y):
    return (y + H0) * XE0 + x + H0


def lane1(x, y):
    return (y + H1) * XE1 + x + H1


def tables(nx, ny, nz):
    x2, y2 = 2 * nx, 4 * ny
    l2, l3 = up128(x2 * y2), up128(nx * 2 * ny)
    t = {}
    place0 = np.zeros((512, L0), np.float32)
    sel0 = np.zeros((32, L0), np.float32)
    unsel = np.zeros((128, L0), np.float32)
    for x in range(8):
        for y in range(16):
            place0[x * 16 + y, lane0(x, y)] = 1
            unsel[x * 16 + y, lane0(x, y)] = 1
            sel0[(x // 2) * 8 + y // 2, lane0(x, y)] = 0.125
    for x in range(8):
        for y in range(16):
            xx, yy = (x + 8 if x < 4 else x - 8), (y + 16 if y < 8 else y - 16)
            place0[128 + x * 16 + y, lane0(xx, y)] = 1
            if -H0 <= yy < 16 + H0:
                place0[256 + x * 16 + y, lane0(x, yy)] = 1
                place0[384 + x * 16 + y, lane0(xx, yy)] = 1
    place1 = np.zeros((384, L1), np.float32)
    for d, (sx, sy) in enumerate([(0, 0)] + DIRS):
        for x in range(4):
            for y in range(8):
                xx, yy = x + 4 * sx, y + 8 * sy
                if -H1 <= xx < 4 + H1 and -H1 <= yy < 8 + H1:
                    place1[32 * d + x * 8 + y, lane1(xx, yy)] = 1
    for e, (sx, sy) in enumerate(FAR):
        for y in range(8):
            xx, yy = (-5 if sx < 0 else 8), y + 8 * sy
            if -H1 <= yy < 8 + H1:
                place1[288 + 8 * e + y, lane1(xx, yy)] = 1
    sel1 = np.zeros((8, L1), np.float32)
    quarter = np.zeros((8, L1), np.float32)
    for x in range(4):
        for y in range(8):
            sel1[x // 2, lane1(x, y)] = 0.125
            quarter[y // 2, lane1(x, y)] = 1
    prol0 = np.zeros((L1, L0), np.float32)
    for x in range(-H0, 8 + H0):
        for y in range(-H0, 16 + H0):
            prol0[lane1(x // 2, y // 2), lane0(x, y)] = 1
    perm2 = np.zeros((nx * ny * 8, l2), np.float32)
    for a in range(nx):
        for b in range(ny):
            for i in range(2):
                for j in range(4):
                    perm2[j * nx * ny * 2 + (a * ny + b) * 2 + i, (b * 4 + j) * x2 + a * 2 + i] = 1
    rest2 = np.zeros((l2, l3), np.float32)
    for x in range(x2):
        for y in range(y2):
            rest2[y * x2 + x, (y // 2) * nx + x // 2] = 0.125
    prol2 = (rest2.T != 0).astype(np.float32)
    kx1 = np.zeros((32, 128), np.float32)
    kx2 = np.zeros((4, 8, 128), np.float32)
    for x in range(8):
        for y in range(16):
            kx1[(x // 2) * 8 + y // 2, x * 16 + y] = 0.25
            kx2[y // 4, x // 4, x * 16 + y] = 0.0625
    kz1 = np.zeros((128, 128), np.float32)
    kz2 = np.zeros((128, 128), np.float32)
    for z in range(128):
        kz1[z, z // 2] = 0.5
        for c in range(4):
            kz2[z, 32 * c + z // 4] = 0.25
    coord = np.full((16, max(L0, l2)), OUT, np.int32)
    for x in range(-H0, 8 + H0):
        for y in range(-H0, 16 + H0):
            coord[0:2, lane0(x, y)] = x, y
    for x in range(-H1, 4 + H1):
        for y in range(-H1, 8 + H1):
            coord[2:4, lane1(x, y)] = x, y
            coord[8, lane1(x, y)] = (y // 2) * x2 + x // 2
    for x in range(x2):
        for y in range(y2):
            coord[4:6, y * x2 + x] = x, y
    for x in range(nx):
        for y in range(2 * ny):
            coord[6:8, y * nx + x] = x, y
            coord[9, y * nx + x] = (x % 2) * ny * nz + (y // 2) * nz
    coord[10:14, 0:L1] = quarter[0:4]
    sel0r = np.concatenate([sel0] * 4, axis=0).T
    names = dict(sel0r=sel0r, place0=place0, sel0=sel0, unsel=unsel, place1=place1, sel1=sel1, prol0=prol0, perm2=perm2, rest2=rest2,
                 prol2=prol2, kx1=kx1, kx2=kx2.reshape(32, 128), kz1=kz1, kz2=kz2)
    t = {k: v.astype(jnp.bfloat16) for k, v in names.items()}
    t["coord"] = coord
    return t


def split(x):
    hi = x.astype(BF16)
    return hi, (x - hi.astype(F32)).astype(BF16)


def times(x, w):
    rows = x.shape[0]
    both = jnp.dot(jnp.concatenate(split(x), axis=0), w, preferred_element_type=F32)
    return both[:rows] + both[rows:]


def select_t(w, x):
    dims = (((1,), (1,)), ((), ()))
    hi, lo = split(x)
    return lax.dot_general(w, hi, dims, preferred_element_type=F32) + lax.dot_general(w, lo, dims, preferred_element_type=F32)


def left(w, x):
    hi, lo = split(x)
    return jnp.dot(w, hi, preferred_element_type=F32) + jnp.dot(w, lo, preferred_element_type=F32)


def build(nx, ny, nz):
    x2, y2 = 2 * nx, 4 * ny
    l2, l3 = up128(x2 * y2), up128(nx * 2 * ny)
    consts = tables(nx, ny, nz)
    names = list(consts)

    n_sem = 3 * 26 + 16 + 2 * 26 + 3 * (3 * ny + nx)

    scratch = dict(
        nat0=pltpu.VMEM((3, 3, 8, 16, 128), F32),
        slab0=pltpu.VMEM((3, 2, 8, 128), F32),
        slabs0=pltpu.VMEM((3, 2, 9, 8, 128), F32),
        rhs0=pltpu.VMEM((R0, L0), F32),
        nat1=pltpu.VMEM((3, 48, 8, 128), F32),
        slab1=pltpu.VMEM((3, 2, 8, 128), F32),
        slabs1=pltpu.VMEM((3, 2, 9, 8, 128), F32),
        ext1=pltpu.VMEM((R1, L1), F32),
        yz2=pltpu.VMEM((3, 3, ny, 2, 128), F32),
        xs2=pltpu.VMEM((3, nx, 3, ny, 2, 128), F32),
        rhs_v=pltpu.VMEM((8, 16, 128), F32),
        coef_v=pltpu.VMEM((8, 16, 128), F32),
        sol=pltpu.VMEM((8, 16, 128), F32),
        m0=pltpu.VMEM((6, R0, L0), F32),
        c0=pltpu.VMEM((4, R0, L0), F32),
        m1=pltpu.VMEM((6, R1, L1), F32),
        c1=pltpu.VMEM((4, R1, L1), F32),
        m2=pltpu.VMEM((6, R2, l2), F32),
        c2=pltpu.VMEM((4, R2, l2), F32),
        m3=pltpu.VMEM((6, R3, l3), F32),
        c3=pltpu.VMEM((2, R3, l3), F32),
        pairs=pltpu.VMEM((max(L0, l2) // 128, 160, 128), F32),
        prol1=pltpu.VMEM((l2, L1), BF16),
        lsem=pltpu.SemaphoreType.DMA((2 + len(names),)),
        ssem=pltpu.SemaphoreType.DMA((n_sem,)),
        rsem=pltpu.SemaphoreType.DMA((n_sem,)),
    )
    keys = list(scratch)
    held = [pltpu.VMEM(consts[k].shape, consts[k].dtype) for k in names]

    def kernel(rhs_hbm, coef_hbm, agg, *rest):
        out = rest[len(names)]
        s = dict(zip(keys, rest[len(names) + 1:]))
        local = dict(zip(names, rest[len(names) + 1 + len(keys):]))
        rhs, coef = s["rhs_v"], s["coef_v"]
        loads = {"rhs": pltpu.make_async_copy(rhs_hbm, rhs, s["lsem"].at[0]), "coef": pltpu.make_async_copy(coef_hbm, coef, s["lsem"].at[1])}
        for i, k in enumerate(names):
            loads[k] = pltpu.make_async_copy(rest[i], local[k], s["lsem"].at[2 + i])
        waited = set()

        def ready(k):
            if k not in waited:
                waited.add(k)
                loads[k].wait()

        class Table:
            def __getitem__(self, k):
                ready(k)
                return local[k]

        c = Table()
        gx, gy, gz = lax.axis_index("gx"), lax.axis_index("gy"), lax.axis_index("gz")

        def has(dx, dy, dz):
            ok = None
            for g, d, n in ((gx, dx, nx), (gy, dy, ny), (gz, dz, nz)):
                if d:
                    here = (g + d >= 0) if d < 0 else (g + d < n)
                    ok = here if ok is None else ok & here
            return ok

        counter = [0]
        unsent = []

        class Copy:
            def __init__(self, src, dst, there, send_if, recv_if):
                i = counter[0]
                counter[0] += 1
                self.make = lambda: pltpu.make_async_remote_copy(
                    src_ref=src, dst_ref=dst, send_sem=s["ssem"].at[i], recv_sem=s["rsem"].at[i],
                    device_id=there, device_id_type=MESH)
                self.send_if, self.recv_if = send_if, recv_if
                unsent.append(self)
                self.started = False

            def under(self, cond, f):
                if cond is None:
                    f()
                else:
                    pl.when(cond)(f)

            def start(self):
                self.started = True
                self.under(self.send_if, lambda: self.make().start())

            def arrive(self):
                self.under(self.recv_if, lambda: self.make().wait_recv())

            def sent(self):
                self.under(self.send_if, lambda: self.make().wait_send())

        def toward(dx, dy, dz, src, dst):
            return Copy(src, dst, (gx + dx, gy + dy, gz + dz), has(dx, dy, dz), has(-dx, -dy, -dz))

        def halo0(n, src):
            copies = []
            for dx, dy in DIRS:
                xs = slice(0, 8) if dx == 0 else (slice(4, 8) if dx > 0 else slice(0, 4))
                ys = slice(0, 16) if dy == 0 else (slice(8, 16) if dy > 0 else slice(0, 8))
                group = 0 if dy == 0 else (1 if dx == 0 else 2)
                copies.append(toward(dx, dy, 0, src.at[xs, ys, :], s["nat0"].at[n, group, xs, ys, :]))
            return copies

        def slab_halo(n, slab, slabs):
            return [toward(dx, dy, dz, slab.at[n, 0 if dz < 0 else 1], slabs.at[n, 1 if dz < 0 else 0, ALL.index((-dx, -dy))])
                    for dx, dy in reversed(ALL) for dz in (-1, 1)]

        def plane1(n):
            copies = []
            for dx, dy in DIRS:
                d = ALL.index((-dx, -dy))
                copies.append(toward(dx, dy, 0, s["nat1"].at[n, 0:4], s["nat1"].at[n, 4 * d:4 * d + 4]))
            return copies

        def far1(n):
            copies = []
            for dx, dy in FAR:
                e = FAR.index((-dx, -dy))
                i = 3 if dx > 0 else 0
                copies.append(toward(dx, dy, 0, s["nat1"].at[n, i:i + 1], s["nat1"].at[n, 36 + e:37 + e]))
            return copies

        def z_halo1():
            return [toward(0, 0, -1, s["ext1"].at[8:16, :], s["ext1"].at[R1 - 8:R1, :]),
                    toward(0, 0, 1, s["ext1"].at[R1 - 16:R1 - 8, :], s["ext1"].at[0:8, :])]

        def yzline(n):
            mine = s["yz2"].at[n, 1, gy]
            return [Copy(mine, s["yz2"].at[n, 1 - dz, gy], (gx, lax.rem(gy + d, ny), gz + dz), has(0, 0, dz), has(0, 0, -dz))
                    for d in sorted(range(ny), key=lambda d: -min(d, ny - d)) for dz in (-1, 1, 0) if d or dz]

        def xline(n):
            return [Copy(s["yz2"].at[n], s["xs2"].at[n, gx], (lax.rem(gx + d, nx), gy, gz), None, None)
                    for d in sorted(range(1, nx), key=lambda d: -min(d, nx - d))]

        def start(copies):
            for copy in copies:
                copy.start()

        def arrive(copies):
            done = [copy for copy in unsent if copy.started and copy not in copies]
            for copy in done:
                copy.sent()
                unsent.remove(copy)
            for copy in copies:
                copy.arrive()

        srcs = (rhs, coef, s["sol"])
        srcs = (rhs, coef, s["sol"])
        P0 = [halo0(n, srcs[n]) for n in range(3)]
        S0 = [slab_halo(n, s["slab0"], s["slabs0"]) for n in range(3)]
        P1 = [plane1(n) for n in range(3)]
        S1 = [None] + [slab_halo(n, s["slab1"], s["slabs1"]) for n in (1, 2)]
        F1 = far1(0)
        Z1 = z_halo1()
        Y2 = [yzline(n) for n in range(3)]
        X2 = [xline(n) for n in range(3)]

        barrier = pltpu.get_barrier_semaphore()
        for d in range(1, nx):
            pl.semaphore_signal(barrier, inc=1, device_id=(lax.rem(gx + d, nx), gy, gz), device_id_type=MESH)
        for d in range(1, ny):
            pl.semaphore_signal(barrier, inc=1, device_id=(gx, lax.rem(gy + d, ny), gz), device_id_type=MESH)
        total = jnp.int32(nx - 1 + ny - 1)
        for dz in (-1, 1):
            ok = has(0, 0, dz)
            total = total + ny * ok.astype(jnp.int32)

            @pl.when(ok)
            def _(dz=dz):
                for d in range(ny):
                    pl.semaphore_signal(barrier, inc=1, device_id=(gx, lax.rem(gy + d, ny), gz + dz), device_id_type=MESH)
        near = [(dx, dy, 0) for dx, dy in DIRS + FAR if dx and dy] + [(dx, dy, dz) for dx, dy in DIRS if dx for dz in (-1, 1)]
        for dx, dy, dz in near:
            ok = has(dx, dy, dz)
            total = total + ok.astype(jnp.int32)

            @pl.when(ok)
            def _(dx=dx, dy=dy, dz=dz):
                pl.semaphore_signal(barrier, inc=1, device_id=(gx + dx, gy + dy, gz + dz), device_id_type=MESH)

        for k in ["coef", "rhs", "kx1", "kx2", "kz1", "kz2", "place0"]:
            loads[k].start()
        for k in names:
            if k not in ("kx1", "kx2", "kz1", "kz2", "place0"):
                loads[k].start()

        def clear(dx, dy, dz, dsts):
            @pl.when(jnp.logical_not(has(dx, dy, dz)))
            def _():
                for ref, index in dsts:
                    ref[index] = jnp.zeros(ref.at[index].shape, F32)

        for dx, dy in DIRS:
            xs = slice(0, 8) if dx == 0 else (slice(4, 8) if dx < 0 else slice(0, 4))
            ys = slice(0, 16) if dy == 0 else (slice(8, 16) if dy < 0 else slice(0, 8))
            group = 0 if dy == 0 else (1 if dx == 0 else 2)
            d = ALL.index((dx, dy))
            dsts = []
            for n in range(3):
                dsts.append((s["nat0"], (n, group, xs, ys)))
                dsts.append((s["nat1"], (n, slice(4 * d, 4 * d + 4))))
                for side in range(2):
                    dsts.append((s["slabs0"], (n, side, d)))
                    if n:
                        dsts.append((s["slabs1"], (n, side, d)))
            clear(dx, dy, 0, dsts)
        for e, (dx, dy) in enumerate(FAR):
            clear(dx, dy, 0, [(s["nat1"], (0, slice(36 + e, 37 + e)))])
        for dz in (-1, 1):
            side = 0 if dz < 0 else 1
            dsts = [(s["ext1"], (slice(0, 8) if dz < 0 else slice(R1 - 8, R1),))]
            for n in range(3):
                dsts.append((s["slabs0"], (n, side)))
                if n:
                    dsts.append((s["slabs1"], (n, side)))
                dsts.append((s["yz2"], (n, 1 + dz)))
            clear(0, 0, dz, dsts)
        s["nat1"][0, 42:48] = jnp.zeros((6, 8, 128), F32)
        for n in (1, 2):
            s["nat1"][n, 36:48] = jnp.zeros((12, 8, 128), F32)

        ready("coef")
        k_nat = coef[...].reshape(128, 128)
        k_flip = k_nat.T
        s["slab0"][1, 0] = k_flip[0:8]
        s["slab0"][1, 1] = k_flip[120:128]
        ready("rhs")
        f_flip = rhs[...].reshape(128, 128).T
        s["slab0"][0, 0] = f_flip[0:8]
        s["slab0"][0, 1] = f_flip[120:128]
        pl.semaphore_wait(barrier, total)
        start(S0[1])
        start(P0[1])
        start(S0[0])
        start(P0[0])
        k1 = times(left(c["kx1"][...], k_nat), c["kz1"][...])
        s["nat1"][0, 0:4] = k1.reshape(4, 8, 128)
        start(P1[0])
        start(F1)
        k2_parts = times(left(c["kx2"][...], k_nat), c["kz2"][...])
        lane = lax.broadcasted_iota(jnp.int32, (8, 128), 1)

        def by_quarter(parts):
            return jnp.where(lane < 32, parts[0], jnp.where(lane < 64, parts[1], jnp.where(lane < 96, parts[2], parts[3])))

        s["yz2"][0, 1, gy] = by_quarter([k2_parts[8 * q:8 * q + 8] for q in range(4)])[0:2]
        start(Y2[0])

        def shifts(v, xe):
            rows, lanes = v.shape
            return (pltpu.roll(v, lanes - 1, 1), pltpu.roll(v, 1, 1), pltpu.roll(v, lanes - xe, 1), pltpu.roll(v, xe, 1),
                    pltpu.roll(v, rows - 1, 0), pltpu.roll(v, 1, 0))

        def setup(k, xe, factor, inside, inner, extra, m, consts_ref):
            rows, lanes = k.shape
            ws = []
            for i, other in enumerate(shifts(k, xe)):
                if inner is not None and i < 4:
                    other = jnp.where(inner[i], other, 0.0)
                ws.append(0.5 * (k + other))
            diag = ws[0]
            for w in ws[1:]:
                diag = diag + w
            diag = factor * diag
            minv = jnp.where(inside, 0.8 / diag, 0.0)
            for i, w in enumerate(ws):
                link = (factor * minv) * w
                if inner is not None and i < 4:
                    link = jnp.where(inner[i], link, 0.0)
                if extra is not None:
                    link = jnp.where(extra[i], link, 0.0)
                m[i] = link
            consts_ref[0] = minv
            if consts_ref.shape[0] > 2:
                consts_ref[1] = 1.25 * diag

        def sweep(v, g, m, xe):
            total = 0.2 * v + g
            for i, other in enumerate(shifts(v, xe)):
                total = total + m[i] * other
            return total

        def coords(level, lanes, rows, x_off, y_off, z_off):
            x = c["coord"][2 * level:2 * level + 1, 0:lanes] + x_off
            y = c["coord"][2 * level + 1:2 * level + 2, 0:lanes] + y_off
            z = lax.broadcasted_iota(jnp.int32, (rows, lanes), 0) + z_off
            return x, y, z

        def inside_of(x, y, z, sizes):
            plane = (x >= 0) & (x < sizes[0]) & (y >= 0) & (y < sizes[1])
            return jnp.broadcast_to(plane, z.shape) & (z >= 0) & (z < sizes[2])

        def assemble0(n, flipped):
            blocks = [flipped] + [s["nat0"][n, i].reshape(128, 128).T for i in range(3)]
            right = lane < 64
            above = lax.rem(lane, 16) < 8
            ends = []
            for side in range(2):
                def at(dx, dy, side=side):
                    return s["slabs0"][n, side, ALL.index((dx, dy))]

                ends.append(jnp.concatenate([
                    at(0, 0), jnp.where(right, at(1, 0), at(-1, 0)), jnp.where(above, at(0, 1), at(0, -1)),
                    jnp.where(right, jnp.where(above, at(1, 1), at(1, -1)), jnp.where(above, at(-1, 1), at(-1, -1)))], axis=1))
            wide = jnp.concatenate([ends[0], jnp.concatenate(blocks, axis=1), ends[1]], axis=0)
            return times(wide, c["place0"][...])

        def natural1(n):
            nat = s["nat1"][n].reshape(384, 128)
            return jnp.concatenate([nat[128 * i:128 * i + 128].T for i in range(3)], axis=1)[0:64]

        def assemble1(n):
            ends = []
            for side in range(2):
                slabs = [s["slabs1"][n, side, d] for d in range(9)]
                ends.append(jnp.concatenate([by_quarter(slabs[0:4]), by_quarter(slabs[4:8]), jnp.where(lane < 32, slabs[8], 0.0)], axis=1))
            wide = jnp.concatenate([ends[0], natural1(n), ends[1]], axis=0)
            return times(wide, c["place1"][...])

        def gather2_x(n):
            arrive(Y2[n])
            start(X2[n])
            s["xs2"][n, gx] = s["yz2"][n]

        def gather2(n):
            arrive(X2[n])
            rows = []
            for dz in range(3):
                flipped = s["xs2"][n, :, dz].reshape(nx * ny * 2, 128).T
                rows.append(jnp.concatenate([flipped[32 * q:32 * q + 32] for q in range(4)], axis=1))
            return times(jnp.concatenate(rows, axis=0), c["perm2"][...])

        x1, y1, z1 = coords(1, L1, R1, 4 * gx, 8 * gy, 64 * gz - 8)
        target = c["coord"][8:9, 0:L1] + (2 * gx + 4 * gy * x2)
        target = jnp.where((x1 >= 0) & (x1 < 4 * nx) & (y1 >= 0) & (y1 < 8 * ny), target, -1)
        s["prol1"][...] = jnp.where(lax.broadcasted_iota(jnp.int32, (l2, L1), 0) == target, 1.0, 0.0).astype(BF16)

        near_owner = []
        xb = c["coord"][6:7, 0:l3]
        for i in (jnp.maximum(gz - 1, 0), gz, jnp.minimum(gz + 1, nz - 1)):
            pick = lax.broadcasted_iota(jnp.int32, (2 * ny * nz, l3), 0) == c["coord"][9:10, 0:l3] + i
            picked = jnp.dot(agg[...].astype(F32).astype(BF16), jnp.where(pick, 1.0, 0.0).astype(BF16), preferred_element_type=F32)
            mine = jnp.zeros((1, l3), F32)
            for r in range(nx // 2):
                mine = jnp.where(xb // 2 == r, picked[r:r + 1], mine)
            near_owner.append(jnp.broadcast_to(mine, (16, l3)))
        owner = jnp.concatenate(near_owner, axis=0)

        arrive(P1[0] + F1)
        s["ext1"][8:R1 - 8] = times(natural1(0), c["place1"][...])
        start(Z1)

        arrive(P0[1] + S0[1])
        k0 = assemble0(1, k_flip)
        x0, y0, z0 = coords(0, L0, R0, 8 * gx, 16 * gy, 128 * gz - 8)
        setup(k0, XE0, 1.0, inside_of(x0, y0, z0, (8 * nx, 16 * ny, 128 * nz)), None, None, s["m0"], s["c0"])
        arrive(P0[0] + S0[0])
        f0 = assemble0(0, f_flip)
        s["rhs0"][...] = f0
        s["c0"][2] = s["c0"][0] * f0

        def halved(v, first, half):
            rows, lanes = v.shape
            sums = []
            for j in range(lanes // 128):
                s["pairs"][j, 0:rows] = v[:, 128 * j:128 * j + 128]
                sums.append(s["pairs"][j, pl.ds(first, half, stride=2), :] + s["pairs"][j, pl.ds(first + 1, half, stride=2), :])
            return sums[0] if len(sums) == 1 else jnp.concatenate(sums, axis=1)

        def doubled(v, first, rows):
            half, lanes = v.shape
            parts = []
            for j in range(lanes // 128):
                part = v[:, 128 * j:128 * j + 128]
                s["pairs"][j, pl.ds(0, half, stride=2), :] = part
                s["pairs"][j, pl.ds(1, half, stride=2), :] = part
                parts.append(s["pairs"][j, first:first + rows])
            return parts[0] if len(parts) == 1 else jnp.concatenate(parts, axis=1)

        def down(m, consts_ref, xe):
            g = consts_ref[2]
            v = sweep(g, g, m, xe)
            consts_ref[3] = v
            return v

        def residual(v, g, m, consts_ref, xe):
            return consts_ref[1] * (sweep(v, g, m, xe) - v)

        for cycle in range(2):
            n = 1 + cycle
            v = down(s["m0"], s["c0"], XE0)
            r = residual(v, s["c0"][2], s["m0"], s["c0"], XE0)
            half = halved(r, 8, 64)
            ends = times(jnp.concatenate([half[0:8], half[56:64]], axis=0), c["sel0r"][...])
            s["slab1"][n] = ends.reshape(2, 8, 128)
            start(S1[n])
            s["nat1"][n, 0:4, :, 0:64] = select_t(c["sel0"][...], half).reshape(4, 8, 64)
            start(P1[n])
            if cycle == 0:
                gather2_x(0)
                arrive(Z1)
                inside = inside_of(x1, y1, z1, (4 * nx, 8 * ny, 64 * nz))
                setup(s["ext1"][...], XE1, 0.25, inside, None, None, s["m1"], s["c1"])
            arrive(P1[n] + S1[n])
            s["c1"][2] = s["c1"][0] * assemble1(n)
            v = down(s["m1"], s["c1"], XE1)
            half = halved(residual(v, s["c1"][2], s["m1"], s["c1"], XE1), 8, 32)
            quarters = [jnp.where(c["coord"][10 + q:11 + q, 0:L1] > 0, half, 0.0) for q in range(4)]
            s["yz2"][n, 1, gy] = select_t(c["sel1"][...], jnp.concatenate(quarters, axis=0))[0:2]
            start(Y2[n])
            if cycle == 0:
                k2 = gather2(0)
                x, y, z = coords(2, l2, R2, 0, 0, 32 * gz - 32)
                inner = [jnp.broadcast_to(q, z.shape) for q in (x + 1 < x2, x > 0, y + 1 < y2, y > 0)]
                setup(k2, x2, 0.0625, inside_of(x, y, z, (x2, y2, 32 * nz)), inner, None, s["m2"], s["c2"])
                k3 = times(halved(k2, 0, R3), c["rest2"][...])
                x, y, z = coords(3, l3, R3, 0, 0, 16 * gz - 16)
                inner = [jnp.broadcast_to(q, z.shape) for q in (x + 1 < nx, x > 0, y + 1 < 2 * ny, y > 0)]
                same = [other == owner for other in shifts(owner, nx)]
                setup(k3, nx, 0.015625, inside_of(x, y, z, (nx, 2 * ny, 16 * nz)), inner, same, s["m3"], s["c3"])
            gather2_x(n)
            f2 = gather2(n)
            s["c2"][2] = s["c2"][0] * f2
            v2 = down(s["m2"], s["c2"], x2)
            r = residual(v2, s["c2"][2], s["m2"], s["c2"], x2)
            g3 = s["c3"][0] * times(halved(r, 0, R3), c["rest2"][...])
            e = g3
            for j in range(COARSE_SWEEPS - 1):
                e = sweep(e, g3, s["m3"], nx)
            fine = times(e, c["prol2"][...])
            v = s["c2"][3] + doubled(fine, 0, R2)
            for j in range(2):
                v = sweep(v, s["c2"][2], s["m2"], x2)
            fine = times(v[24:72], s["prol1"][...])
            v = s["c1"][3] + doubled(fine, 8, R1)
            for j in range(2):
                v = sweep(v, s["c1"][2], s["m1"], XE1)
            fine = times(v, c["prol0"][...])
            v = s["c0"][3] + doubled(fine, 8, R0)
            for j in range(2):
                v = sweep(v, s["c0"][2], s["m0"], XE0)
            nat = select_t(c["unsel"][...], v[8:R0 - 8])
            if cycle == 0:
                s["sol"][...] = nat.reshape(8, 16, 128)
                flipped = nat.T
                s["slab0"][2, 0] = flipped[0:8]
                s["slab0"][2, 1] = flipped[120:128]
                start(S0[2])
                start(P0[2])
                arrive(P0[2] + S0[2])
                now = assemble0(2, flipped)
                s["c0"][2] = sweep(now, s["c0"][0] * s["rhs0"][...], s["m0"], XE0) - now
            else:
                out[...] = s["sol"][...] + nat.reshape(8, 16, 128)
        for k in loads:
            ready(k)
        for copy in unsent:
            copy.sent()

    vmem = pl.BlockSpec(memory_space=pltpu.VMEM)
    hbm = pl.BlockSpec(memory_space=pl.ANY)

    def body(rhs, coef, agglom):
        agg = agglom.reshape(nx // 2, 2 * ny * nz)
        return pl.pallas_call(
            kernel,
            out_shape=pltpu.VMEM((8, 16, 128), F32),
            in_specs=[hbm, hbm, vmem] + [hbm] * len(names),
            out_specs=vmem,
            scratch_shapes=[scratch[k] for k in keys] + held,
            compiler_params=pltpu.CompilerParams(collective_id=0, has_side_effects=True, vmem_limit_bytes=60 * 1024 * 1024),
        )(rhs, coef, agg, *[jnp.asarray(consts[k]) for k in names])

    return body


def solution(mesh):
    body = build(mesh.shape["gx"], mesh.shape["gy"], mesh.shape["gz"])
    spec = P("gx", "gy", "gz")
    return jax.shard_map(body, mesh=mesh, in_specs=(spec, spec, P()), out_specs=spec, check_vma=False)
```

```python
import jax
import jax.numpy as jnp
import numpy as np
from jax import lax
from jax.experimental import pallas as pl
from jax.experimental.pallas import tpu as pltpu
from jax.sharding import PartitionSpec as P

F32 = jnp.float32
BF16 = jnp.bfloat16
MESH = pl.DeviceIdType.MESH
OUT = -100000
COARSE_SWEEPS = 8
DIRS = [(dx, dy) for dx in (-1, 0, 1) for dy in (-1, 0, 1) if (dx, dy) != (0, 0)]
ALL = [(0, 0)] + DIRS
FAR = [(dx, dy) for dx in (-2, 2) for dy in (-1, 0, 1)]
XE0, YE0, H0 = 16, 24, 4
XE1, YE1, H1 = 14, 18, 5
L0, L1 = 384, 256
R0, R1, R2, R3 = 144, 80, 96, 48


def up128(n):
    return -(-n // 128) * 128


def lane0(x, y):
    return (y + H0) * XE0 + x + H0


def lane1(x, y):
    return (y + H1) * XE1 + x + H1


def tables(nx, ny, nz):
    x2, y2 = 2 * nx, 4 * ny
    l2, l3 = up128(x2 * y2), up128(nx * 2 * ny)
    t = {}
    place0 = np.zeros((384, L0), np.float32)
    sel0 = np.zeros((32, L0), np.float32)
    unsel = np.zeros((128, L0), np.float32)
    for x in range(8):
        for y in range(16):
            place0[x * 16 + y, lane0(x, y)] = 1
            unsel[x * 16 + y, lane0(x, y)] = 1
            sel0[(x // 2) * 8 + y // 2, lane0(x, y)] = 0.125
    for x in range(8):
        for y in range(16):
            place0[128 + x * 16 + y, lane0(x + 8 if x < 4 else x - 8, y)] = 1
        for yi in range(H0):
            place0[256 + x * 4 + yi, lane0(x, yi - H0)] = 1
            place0[288 + x * 4 + yi, lane0(x, yi + 16)] = 1
            if x >= 4:
                place0[320 + (x - 4) * 4 + yi, lane0(x - 8, yi - H0)] = 1
                place0[336 + (x - 4) * 4 + yi, lane0(x - 8, yi + 16)] = 1
            else:
                place0[352 + x * 4 + yi, lane0(x + 8, yi - H0)] = 1
                place0[368 + x * 4 + yi, lane0(x + 8, yi + 16)] = 1
    place1 = np.zeros((384, L1), np.float32)
    for d, (sx, sy) in enumerate([(0, 0)] + DIRS):
        for x in range(4):
            for y in range(8):
                xx, yy = x + 4 * sx, y + 8 * sy
                if -H1 <= xx < 4 + H1 and -H1 <= yy < 8 + H1:
                    place1[32 * d + x * 8 + y, lane1(xx, yy)] = 1
    for e, (sx, sy) in enumerate(FAR):
        for y in range(8):
            xx, yy = (-5 if sx < 0 else 8), y + 8 * sy
            if -H1 <= yy < 8 + H1:
                place1[288 + 8 * e + y, lane1(xx, yy)] = 1
    sel1 = np.zeros((8, L1), np.float32)
    quarter = np.zeros((8, L1), np.float32)
    for x in range(4):
        for y in range(8):
            sel1[x // 2, lane1(x, y)] = 0.125
            quarter[y // 2, lane1(x, y)] = 1
    prol0 = np.zeros((L1, L0), np.float32)
    for x in range(-H0, 8 + H0):
        for y in range(-H0, 16 + H0):
            prol0[lane1(x // 2, y // 2), lane0(x, y)] = 1
    perm2 = np.zeros((nx * ny * 8, l2), np.float32)
    for a in range(nx):
        for b in range(ny):
            for i in range(2):
                for j in range(4):
                    perm2[j * nx * ny * 2 + (a * ny + b) * 2 + i, (b * 4 + j) * x2 + a * 2 + i] = 1
    rest2 = np.zeros((l2, l3), np.float32)
    for x in range(x2):
        for y in range(y2):
            rest2[y * x2 + x, (y // 2) * nx + x // 2] = 0.125
    prol2 = (rest2.T != 0).astype(np.float32)
    kx1 = np.zeros((32, 128), np.float32)
    kx2 = np.zeros((4, 8, 128), np.float32)
    for x in range(8):
        for y in range(16):
            kx1[(x // 2) * 8 + y // 2, x * 16 + y] = 0.25
            kx2[y // 4, x // 4, x * 16 + y] = 0.0625
    kz1 = np.zeros((128, 128), np.float32)
    kz2 = np.zeros((128, 128), np.float32)
    for z in range(128):
        kz1[z, z // 2] = 0.5
        for c in range(4):
            kz2[z, 32 * c + z // 4] = 0.25
    coord = np.full((16, max(L0, l2)), OUT, np.int32)
    for x in range(-H0, 8 + H0):
        for y in range(-H0, 16 + H0):
            coord[0:2, lane0(x, y)] = x, y
    for x in range(-H1, 4 + H1):
        for y in range(-H1, 8 + H1):
            coord[2:4, lane1(x, y)] = x, y
            coord[8, lane1(x, y)] = (y // 2) * x2 + x // 2
    for x in range(x2):
        for y in range(y2):
            coord[4:6, y * x2 + x] = x, y
    for x in range(nx):
        for y in range(2 * ny):
            coord[6:8, y * nx + x] = x, y
            coord[9, y * nx + x] = (x % 2) * ny * nz + (y // 2) * nz
    coord[10:14, 0:L1] = quarter[0:4]
    sel0r = np.concatenate([sel0] * 4, axis=0).T
    names = dict(sel0r=sel0r, place0=place0, sel0=sel0, unsel=unsel, place1=place1, sel1=sel1, prol0=prol0, perm2=perm2, rest2=rest2,
                 prol2=prol2, kx1=kx1, kx2=kx2.reshape(32, 128), kz1=kz1, kz2=kz2)
    t = {k: v.astype(jnp.bfloat16) for k, v in names.items()}
    t["coord"] = coord
    return t


def split(x):
    hi = x.astype(BF16)
    return hi, (x - hi.astype(F32)).astype(BF16)


def times(x, w):
    rows = x.shape[0]
    both = jnp.dot(jnp.concatenate(split(x), axis=0), w, preferred_element_type=F32)
    return both[:rows] + both[rows:]


def select_t(w, x):
    dims = (((1,), (1,)), ((), ()))
    hi, lo = split(x)
    return lax.dot_general(w, hi, dims, preferred_element_type=F32) + lax.dot_general(w, lo, dims, preferred_element_type=F32)


def left(w, x):
    hi, lo = split(x)
    return jnp.dot(w, hi, preferred_element_type=F32) + jnp.dot(w, lo, preferred_element_type=F32)


def build(nx, ny, nz):
    x2, y2 = 2 * nx, 4 * ny
    l2, l3 = up128(x2 * y2), up128(nx * 2 * ny)
    consts = tables(nx, ny, nz)
    names = list(consts)

    n_sem = 13

    scratch = dict(
        x0=pltpu.VMEM((3, 8, 16, 128), F32),
        pack0=pltpu.VMEM((3, 8, 8, 128), F32),
        y0=pltpu.VMEM((3, 16, 8, 128), F32),
        slab0=pltpu.VMEM((3, 2, 2, 8, 128), F32),
        slabs0=pltpu.VMEM((3, 2, 9, 8, 128), F32),
        rhs0=pltpu.VMEM((R0, L0), F32),
        nat1=pltpu.VMEM((3, 48, 8, 128), F32),
        slab1=pltpu.VMEM((3, 2, 8, 128), F32),
        slabs1=pltpu.VMEM((3, 2, 9, 8, 128), F32),
        ext1=pltpu.VMEM((R1, L1), F32),
        yz2=pltpu.VMEM((3, 3, ny, 2, 128), F32),
        xs2=pltpu.VMEM((3, nx, 3, ny, 2, 128), F32),
        cells=pltpu.VMEM((3, 8, 16, 128), F32),
        m0=pltpu.VMEM((6, R0, L0), F32),
        c0=pltpu.VMEM((4, R0, L0), F32),
        m1=pltpu.VMEM((6, R1, L1), F32),
        c1=pltpu.VMEM((4, R1, L1), F32),
        m2=pltpu.VMEM((6, R2, l2), F32),
        c2=pltpu.VMEM((4, R2, l2), F32),
        m3=pltpu.VMEM((6, R3, l3), F32),
        c3=pltpu.VMEM((2, R3, l3), F32),
        pairs=pltpu.VMEM((max(L0, l2) // 128, 160, 128), F32),
        agg=pltpu.VMEM((nx // 2, 2 * ny * nz), jnp.int32),
        prol1=pltpu.VMEM((l2, L1), BF16),
        zero16=pltpu.VMEM((2, 4, 16, 128), F32),
        zero8=pltpu.VMEM((2, 4, 8, 128), F32),
        zero2=pltpu.VMEM((2, 128), F32),
        zero_w=pltpu.VMEM((8, L1), F32),
        void8=pltpu.VMEM((104, 8, 128), F32),
        void2=pltpu.VMEM((max(nx, 2) * 3 * ny, 2, 128), F32),
        lsem=pltpu.SemaphoreType.DMA((4,)),
        ssem=pltpu.SemaphoreType.DMA((n_sem,)),
        rsem=pltpu.SemaphoreType.DMA((n_sem,)),
    )
    keys = list(scratch)
    held = [pltpu.VMEM(consts[k].shape, consts[k].dtype) for k in names]

    def kernel(rhs_hbm, coef_hbm, agg_hbm, *rest):
        out = rest[len(names)]
        s = dict(zip(keys, rest[len(names) + 1:]))
        local = dict(zip(names, rest[len(names) + 1 + len(keys):]))
        rhs, coef = s["cells"].at[0], s["cells"].at[1]
        early = ["kx1", "kx2", "kz1", "kz2", "coord"]
        late = [k for k in names if k not in early]
        sources = dict(zip(names, rest))
        loads = {"rhs": [(rhs_hbm, rhs)], "coef": [(coef_hbm, coef)],
                 "early": [(sources[k], local[k]) for k in early] + [(agg_hbm, s["agg"])], "late": [(sources[k], local[k]) for k in late]}
        loads = {k: [pltpu.make_async_copy(a, b, s["lsem"].at[i]) for a, b in pairs] for i, (k, pairs) in enumerate(loads.items())}
        waited = set()

        def ready(k):
            if k not in waited:
                waited.add(k)
                for load in loads[k]:
                    load.wait()

        class Table:
            def __getitem__(self, k):
                ready("early" if k in early else "late")
                return local[k]

        c = Table()
        gx, gy, gz = lax.axis_index("gx"), lax.axis_index("gy"), lax.axis_index("gz")

        def has(dx, dy, dz):
            ok = None
            for g, d, n in ((gx, dx, nx), (gy, dy, ny), (gz, dz, nz)):
                if d:
                    here = (g + d >= 0) if d < 0 else (g + d < n)
                    ok = here if ok is None else ok & here
            return ok

        stages = [0]
        absent = {}

        class Copy:
            def __init__(self, src, dst, there, send_if):
                i = stages[0]
                self.make = lambda: pltpu.make_async_remote_copy(
                    src_ref=src, dst_ref=dst, send_sem=s["ssem"].at[i], recv_sem=s["rsem"].at[i],
                    device_id=there, device_id_type=MESH)
                self.send_if = send_if

            def under(self, f):
                if self.send_if is None:
                    f()
                else:
                    pl.when(self.send_if)(f)

            def start(self):
                self.under(lambda: self.make().start())

            def sent(self):
                self.under(lambda: self.make().wait_send())

        def toward(dx, dy, dz, src, dst, zero):
            i = stages[0]
            absent.setdefault((-dx, -dy, -dz), []).append(lambda: pltpu.make_async_copy(zero, dst, s["rsem"].at[i]).start())
            return Copy(src, dst, (gx + dx, gy + dy, gz + dz), has(dx, dy, dz))

        class Stage:
            def __init__(self, make, void, size):
                self.copies = make()
                self.i, self.void, self.size = stages[0], void, size
                stages[0] += 1

            def start(self):
                for copy in self.copies:
                    copy.start()

            def drain(self):
                for copy in self.copies:
                    copy.sent()

            def arrive(self):
                all_of_it = self.void.at[0:self.size]
                pltpu.make_async_copy(all_of_it, all_of_it, s["rsem"].at[self.i]).wait()

        def halo0(n):
            fields = 2 if n.start == 0 else 1
            copies = []
            for dx, dy in DIRS:
                if dy == 0:
                    xs = slice(4, 8) if dx > 0 else slice(0, 4)
                    copies.append(toward(dx, dy, 0, s["cells"].at[n, xs], s["x0"].at[n, xs], s["zero16"].at[0:fields]))
                    continue
                face = 0 if dy > 0 else 4
                if dx == 0:
                    mine, to = slice(face, face + 4), slice(face, face + 4)
                else:
                    mine = slice(face + 2, face + 4) if dx > 0 else slice(face, face + 2)
                    first = (8 if dx > 0 else 12) + (0 if dy > 0 else 2)
                    to = slice(first, first + 2)
                copies.append(toward(dx, dy, 0, s["pack0"].at[n, mine], s["y0"].at[n, to], s["zero8"].at[0:fields, 0:to.stop - to.start]))
            return copies

        def slab_halo(slab, slabs, zero):
            return [toward(dx, dy, dz, slab(0 if dz < 0 else 1, dy), slabs(1 if dz < 0 else 0, ALL.index((-dx, -dy))), zero)
                    for dx, dy in reversed(ALL) for dz in (-1, 1)]

        def plane1(n):
            copies = []
            for dx, dy in DIRS:
                d = ALL.index((-dx, -dy))
                copies.append(toward(dx, dy, 0, s["nat1"].at[n, 0:4], s["nat1"].at[n, 4 * d:4 * d + 4], s["zero8"].at[0]))
            return copies

        def far1(n):
            copies = []
            for dx, dy in FAR:
                e = FAR.index((-dx, -dy))
                i = 3 if dx > 0 else 0
                copies.append(toward(dx, dy, 0, s["nat1"].at[n, i:i + 1], s["nat1"].at[n, 36 + e:37 + e], s["zero8"].at[0, 0:1]))
            return copies

        def z_halo1():
            return [toward(0, 0, -1, s["ext1"].at[8:16, :], s["ext1"].at[R1 - 8:R1, :], s["zero_w"]),
                    toward(0, 0, 1, s["ext1"].at[R1 - 16:R1 - 8, :], s["ext1"].at[0:8, :], s["zero_w"])]

        def yzline(n):
            mine = s["yz2"].at[n, 1, gy]
            copies = []
            for d in sorted(range(ny), key=lambda d: -min(d, ny - d)):
                for dz in (-1, 1, 0):
                    if d or dz:
                        copies.append(Copy(mine, s["yz2"].at[n, 1 - dz, gy], (gx, lax.rem(gy + d, ny), gz + dz), has(0, 0, dz)))
            i = stages[0]
            for dz in (-1, 1):
                for d in range(ny):
                    absent.setdefault((0, 0, dz), []).append(
                        lambda dz=dz, d=d: pltpu.make_async_copy(s["zero2"], s["yz2"].at[n, 1 + dz, d], s["rsem"].at[i]).start())
            return copies

        def xline(n):
            return [Copy(s["yz2"].at[n], s["xs2"].at[n, gx], (lax.rem(gx + d, nx), gy, gz), None)
                    for d in sorted(range(1, nx), key=lambda d: -min(d, nx - d))]

        E0, E1, Y2, X2 = {}, [], [], []
        for first, fields in ((0, 2), (2, 1)):
            n = slice(first, first + fields)
            E0[first] = Stage(lambda: halo0(n) + slab_halo(lambda side, dy: s["slab0"].at[n, side, 1 if dy else 0],
                                                           lambda side, d: s["slabs0"].at[n, side, d], s["zero8"].at[0:fields, 0]),
                              s["void8"], 50 * fields)
        for n in range(3):
            if n:
                E1.append(Stage(lambda: slab_halo(lambda side, dy: s["slab1"].at[n, side], lambda side, d: s["slabs1"].at[n, side, d],
                                                  s["zero8"].at[0, 0]) + plane1(n), s["void8"], 50))
            else:
                E1.append(Stage(lambda: plane1(0) + far1(0), s["void8"], 38))
            Y2.append(Stage(lambda: yzline(n), s["void2"], 3 * ny - 1))
            X2.append(Stage(lambda: xline(n), s["void2"], (nx - 1) * 3 * ny))
        Z1 = Stage(z_halo1, s["void8"], 4)

        for k in ("zero16", "zero8", "zero2", "zero_w"):
            s[k][...] = jnp.zeros(s[k].shape, F32)

        barrier = pltpu.get_barrier_semaphore()
        for d in range(1, nx):
            pl.semaphore_signal(barrier, inc=1, device_id=(lax.rem(gx + d, nx), gy, gz), device_id_type=MESH)
        for d in range(1, ny):
            pl.semaphore_signal(barrier, inc=1, device_id=(gx, lax.rem(gy + d, ny), gz), device_id_type=MESH)
        total = jnp.int32(nx - 1 + ny - 1)
        for dz in (-1, 1):
            ok = has(0, 0, dz)
            total = total + ny * ok.astype(jnp.int32)

            @pl.when(ok)
            def _(dz=dz):
                for d in range(ny):
                    pl.semaphore_signal(barrier, inc=1, device_id=(gx, lax.rem(gy + d, ny), gz + dz), device_id_type=MESH)
        near = [(dx, dy, 0) for dx, dy in DIRS + FAR if dx and dy] + [(dx, dy, dz) for dx, dy in DIRS if dx for dz in (-1, 1)]
        for dx, dy, dz in near:
            ok = has(dx, dy, dz)
            total = total + ok.astype(jnp.int32)

            @pl.when(ok)
            def _(dx=dx, dy=dy, dz=dz):
                pl.semaphore_signal(barrier, inc=1, device_id=(gx + dx, gy + dy, gz + dz), device_id_type=MESH)

        for k in ("coef", "rhs", "early", "late"):
            for load in loads[k]:
                load.start()

        for place, fills in absent.items():
            @pl.when(jnp.logical_not(has(*place)))
            def _(fills=fills):
                for fill in fills:
                    fill()

        s["nat1"][0, 42:48] = jnp.zeros((6, 8, 128), F32)
        for n in (1, 2):
            s["nat1"][n, 36:48] = jnp.zeros((12, 8, 128), F32)

        def post0(n, nat, flipped):
            cells = nat.reshape(8, 16, 128)
            high, low = cells[:, 12:16].reshape(32, 128), cells[:, 0:4].reshape(32, 128)
            s["pack0"][n, 0:4] = high.reshape(4, 8, 128)
            s["pack0"][n, 4:8] = low.reshape(4, 8, 128)
            faces = jnp.concatenate([high, low, high[16:32], low[16:32], high[0:16], low[0:16]], axis=0).T
            for kind, rows in enumerate((flipped, faces)):
                s["slab0"][n, 0, kind] = rows[0:8]
                s["slab0"][n, 1, kind] = rows[120:128]

        lane = lax.broadcasted_iota(jnp.int32, (8, 128), 1)

        def by_quarter(parts):
            return jnp.where(lane < 32, parts[0], jnp.where(lane < 64, parts[1], jnp.where(lane < 96, parts[2], parts[3])))

        ready("coef")
        k_nat = coef[...].reshape(128, 128)
        k_flip = k_nat.T
        post0(1, k_nat, k_flip)
        ready("rhs")
        f_nat = rhs[...].reshape(128, 128)
        f_flip = f_nat.T
        post0(0, f_nat, f_flip)
        k1 = times(left(c["kx1"][...], k_nat), c["kz1"][...])
        s["nat1"][0, 0:4] = k1.reshape(4, 8, 128)
        k2_parts = times(left(c["kx2"][...], k_nat), c["kz2"][...])
        s["yz2"][0, 1, gy] = by_quarter([k2_parts[8 * q:8 * q + 8] for q in range(4)])[0:2]

        pl.semaphore_wait(barrier, total)
        E0[0].start()
        E1[0].start()
        Y2[0].start()

        def shifts(v, xe):
            rows, lanes = v.shape
            return (pltpu.roll(v, lanes - 1, 1), pltpu.roll(v, 1, 1), pltpu.roll(v, lanes - xe, 1), pltpu.roll(v, xe, 1),
                    pltpu.roll(v, rows - 1, 0), pltpu.roll(v, 1, 0))

        def setup(k, xe, factor, inside, inner, extra, m, consts_ref):
            rows, lanes = k.shape
            ws = []
            for i, other in enumerate(shifts(k, xe)):
                if inner is not None and i < 4:
                    other = jnp.where(inner[i], other, 0.0)
                ws.append(0.5 * (k + other))
            diag = ws[0]
            for w in ws[1:]:
                diag = diag + w
            diag = factor * diag
            minv = jnp.where(inside, 0.8 / diag, 0.0)
            for i, w in enumerate(ws):
                link = (factor * minv) * w
                if inner is not None and i < 4:
                    link = jnp.where(inner[i], link, 0.0)
                if extra is not None:
                    link = jnp.where(extra[i], link, 0.0)
                m[i] = link
            consts_ref[0] = minv
            if consts_ref.shape[0] > 2:
                consts_ref[1] = 1.25 * diag

        def sweep(v, g, m, xe):
            total = 0.2 * v + g
            for i, other in enumerate(shifts(v, xe)):
                total = total + m[i] * other
            return total

        def coords(level, lanes, rows, x_off, y_off, z_off):
            x = c["coord"][2 * level:2 * level + 1, 0:lanes] + x_off
            y = c["coord"][2 * level + 1:2 * level + 2, 0:lanes] + y_off
            z = lax.broadcasted_iota(jnp.int32, (rows, lanes), 0) + z_off
            return x, y, z

        def inside_of(x, y, z, sizes):
            plane = (x >= 0) & (x < sizes[0]) & (y >= 0) & (y < sizes[1])
            return jnp.broadcast_to(plane, z.shape) & (z >= 0) & (z < sizes[2])

        def assemble0(n, flipped):
            blocks = [flipped, s["x0"][n].reshape(128, 128).T, s["y0"][n].reshape(128, 128).T]
            ends = []
            for side in range(2):
                def at(dx, dy, side=side):
                    return s["slabs0"][n, side, ALL.index((dx, dy))]

                diagonals = jnp.where(lane < 80, at(-1, -1), jnp.where(lane < 96, at(-1, 1), jnp.where(lane < 112, at(1, -1), at(1, 1))))
                ends.append(jnp.concatenate([
                    at(0, 0), jnp.where(lane < 64, at(1, 0), at(-1, 0)),
                    jnp.where(lane < 32, at(0, -1), jnp.where(lane < 64, at(0, 1), diagonals))], axis=1))
            wide = jnp.concatenate([ends[0], jnp.concatenate(blocks, axis=1), ends[1]], axis=0)
            return times(wide, c["place0"][...])

        def natural1(n):
            nat = s["nat1"][n].reshape(384, 128)
            return jnp.concatenate([nat[128 * i:128 * i + 128].T for i in range(3)], axis=1)[0:64]

        def assemble1(n):
            ends = []
            for side in range(2):
                slabs = [s["slabs1"][n, side, d] for d in range(9)]
                ends.append(jnp.concatenate([by_quarter(slabs[0:4]), by_quarter(slabs[4:8]), jnp.where(lane < 32, slabs[8], 0.0)], axis=1))
            wide = jnp.concatenate([ends[0], natural1(n), ends[1]], axis=0)
            return times(wide, c["place1"][...])

        def drain(*done):
            for stage in done:
                stage.drain()

        def gather2_x(n):
            Y2[n].arrive()
            X2[n].start()
            s["xs2"][n, gx] = s["yz2"][n]

        def gather2(n):
            X2[n].arrive()
            rows = []
            for dz in range(3):
                flipped = s["xs2"][n, :, dz].reshape(nx * ny * 2, 128).T
                rows.append(jnp.concatenate([flipped[32 * q:32 * q + 32] for q in range(4)], axis=1))
            return times(jnp.concatenate(rows, axis=0), c["perm2"][...])

        x1, y1, z1 = coords(1, L1, R1, 4 * gx, 8 * gy, 64 * gz - 8)
        target = c["coord"][8:9, 0:L1] + (2 * gx + 4 * gy * x2)
        target = jnp.where((x1 >= 0) & (x1 < 4 * nx) & (y1 >= 0) & (y1 < 8 * ny), target, -1)
        s["prol1"][...] = jnp.where(lax.broadcasted_iota(jnp.int32, (l2, L1), 0) == target, 1.0, 0.0).astype(BF16)

        near_owner = []
        xb = c["coord"][6:7, 0:l3]
        for i in (jnp.maximum(gz - 1, 0), gz, jnp.minimum(gz + 1, nz - 1)):
            pick = lax.broadcasted_iota(jnp.int32, (2 * ny * nz, l3), 0) == c["coord"][9:10, 0:l3] + i
            picked = jnp.dot(s["agg"][...].astype(F32).astype(BF16), jnp.where(pick, 1.0, 0.0).astype(BF16), preferred_element_type=F32)
            mine = jnp.zeros((1, l3), F32)
            for r in range(nx // 2):
                mine = jnp.where(xb // 2 == r, picked[r:r + 1], mine)
            near_owner.append(jnp.broadcast_to(mine, (16, l3)))
        owner = jnp.concatenate(near_owner, axis=0)

        E0[0].arrive()
        k0 = assemble0(1, k_flip)
        x0, y0, z0 = coords(0, L0, R0, 8 * gx, 16 * gy, 128 * gz - 8)
        setup(k0, XE0, 1.0, inside_of(x0, y0, z0, (8 * nx, 16 * ny, 128 * nz)), None, None, s["m0"], s["c0"])
        f0 = assemble0(0, f_flip)
        s["rhs0"][...] = f0
        s["c0"][2] = s["c0"][0] * f0

        def halved(v, first, half):
            rows, lanes = v.shape
            sums = []
            for j in range(lanes // 128):
                s["pairs"][j, 0:rows] = v[:, 128 * j:128 * j + 128]
                sums.append(s["pairs"][j, pl.ds(first, half, stride=2), :] + s["pairs"][j, pl.ds(first + 1, half, stride=2), :])
            return sums[0] if len(sums) == 1 else jnp.concatenate(sums, axis=1)

        def doubled(v, first, rows):
            half, lanes = v.shape
            parts = []
            for j in range(lanes // 128):
                part = v[:, 128 * j:128 * j + 128]
                s["pairs"][j, pl.ds(0, half, stride=2), :] = part
                s["pairs"][j, pl.ds(1, half, stride=2), :] = part
                parts.append(s["pairs"][j, first:first + rows])
            return parts[0] if len(parts) == 1 else jnp.concatenate(parts, axis=1)

        def down(m, consts_ref, xe):
            g = consts_ref[2]
            v = sweep(g, g, m, xe)
            consts_ref[3] = v
            return v

        def residual(v, g, m, consts_ref, xe):
            return consts_ref[1] * (sweep(v, g, m, xe) - v)

        for cycle in range(2):
            n = 1 + cycle
            v = down(s["m0"], s["c0"], XE0)
            r = residual(v, s["c0"][2], s["m0"], s["c0"], XE0)
            half = halved(r, 8, 64)
            ends = times(jnp.concatenate([half[0:8], half[56:64]], axis=0), c["sel0r"][...])
            s["slab1"][n] = ends.reshape(2, 8, 128)
            s["nat1"][n, 0:4, :, 0:64] = select_t(c["sel0"][...], half).reshape(4, 8, 64)
            E1[n].start()
            if cycle == 0:
                E1[0].arrive()
                s["ext1"][8:R1 - 8] = times(natural1(0), c["place1"][...])
                Z1.start()
                gather2_x(0)
                Z1.arrive()
                inside = inside_of(x1, y1, z1, (4 * nx, 8 * ny, 64 * nz))
                setup(s["ext1"][...], XE1, 0.25, inside, None, None, s["m1"], s["c1"])
            if cycle == 1:
                drain(X2[1])
            E1[n].arrive()
            s["c1"][2] = s["c1"][0] * assemble1(n)
            v = down(s["m1"], s["c1"], XE1)
            half = halved(residual(v, s["c1"][2], s["m1"], s["c1"], XE1), 8, 32)
            quarters = [jnp.where(c["coord"][10 + q:11 + q, 0:L1] > 0, half, 0.0) for q in range(4)]
            s["yz2"][n, 1, gy] = select_t(c["sel1"][...], jnp.concatenate(quarters, axis=0))[0:2]
            Y2[n].start()
            if cycle == 0:
                k2 = gather2(0)
                x, y, z = coords(2, l2, R2, 0, 0, 32 * gz - 32)
                inner = [jnp.broadcast_to(q, z.shape) for q in (x + 1 < x2, x > 0, y + 1 < y2, y > 0)]
                setup(k2, x2, 0.0625, inside_of(x, y, z, (x2, y2, 32 * nz)), inner, None, s["m2"], s["c2"])
                k3 = times(halved(k2, 0, R3), c["rest2"][...])
                x, y, z = coords(3, l3, R3, 0, 0, 16 * gz - 16)
                inner = [jnp.broadcast_to(q, z.shape) for q in (x + 1 < nx, x > 0, y + 1 < 2 * ny, y > 0)]
                same = [other == owner for other in shifts(owner, nx)]
                setup(k3, nx, 0.015625, inside_of(x, y, z, (nx, 2 * ny, 16 * nz)), inner, same, s["m3"], s["c3"])
            if cycle == 0:
                drain(E0[0], E1[0], Y2[0], Z1)
            else:
                drain(E0[2])
            gather2_x(n)
            if cycle == 0:
                drain(E1[1], X2[0])
            else:
                drain(E1[2], Y2[2])
            f2 = gather2(n)
            s["c2"][2] = s["c2"][0] * f2
            v2 = down(s["m2"], s["c2"], x2)
            r = residual(v2, s["c2"][2], s["m2"], s["c2"], x2)
            g3 = s["c3"][0] * times(halved(r, 0, R3), c["rest2"][...])
            e = g3
            for j in range(COARSE_SWEEPS - 1):
                e = sweep(e, g3, s["m3"], nx)
            fine = times(e, c["prol2"][...])
            v = s["c2"][3] + doubled(fine, 0, R2)
            for j in range(2):
                v = sweep(v, s["c2"][2], s["m2"], x2)
            fine = times(v[24:72], s["prol1"][...])
            v = s["c1"][3] + doubled(fine, 8, R1)
            for j in range(2):
                v = sweep(v, s["c1"][2], s["m1"], XE1)
            fine = times(v, c["prol0"][...])
            v = s["c0"][3] + doubled(fine, 8, R0)
            for j in range(2):
                v = sweep(v, s["c0"][2], s["m0"], XE0)
            nat = select_t(c["unsel"][...], v[8:R0 - 8])
            if cycle == 0:
                s["cells"][2] = nat.reshape(8, 16, 128)
                flipped = nat.T
                post0(2, nat, flipped)
                E0[2].start()
                drain(Y2[1])
                E0[2].arrive()
                now = assemble0(2, flipped)
                s["c0"][2] = sweep(now, s["c0"][0] * s["rhs0"][...], s["m0"], XE0) - now
            else:
                out[...] = s["cells"][2] + nat.reshape(8, 16, 128)
        for k in loads:
            ready(k)
        X2[2].drain()

    vmem = pl.BlockSpec(memory_space=pltpu.VMEM)
    hbm = pl.BlockSpec(memory_space=pl.ANY)

    def body(rhs, coef, agglom):
        agg = agglom.reshape(nx // 2, 2 * ny * nz)
        return pl.pallas_call(
            kernel,
            out_shape=pltpu.VMEM((8, 16, 128), F32),
            in_specs=[hbm, hbm, hbm] + [hbm] * len(names),
            out_specs=vmem,
            scratch_shapes=[scratch[k] for k in keys] + held,
            compiler_params=pltpu.CompilerParams(collective_id=0, has_side_effects=True, vmem_limit_bytes=60 * 1024 * 1024),
        )(rhs, coef, agg, *[jnp.asarray(consts[k]) for k in names])

    return body


def solution(mesh):
    body = build(mesh.shape["gx"], mesh.shape["gy"], mesh.shape["gz"])
    spec = P("gx", "gy", "gz")
    return jax.shard_map(body, mesh=mesh, in_specs=(spec, spec, P()), out_specs=spec, check_vma=False)
```

```python
import jax
import jax.numpy as jnp
import numpy as np
from jax import lax
from jax.experimental import pallas as pl
from jax.experimental.pallas import tpu as pltpu
from jax.sharding import PartitionSpec as P

F32 = jnp.float32
BF16 = jnp.bfloat16
MESH = pl.DeviceIdType.MESH
OUT = -100000
COARSE_SWEEPS = 8
DIRS = [(dx, dy) for dx in (-1, 0, 1) for dy in (-1, 0, 1) if (dx, dy) != (0, 0)]
ALL = [(0, 0)] + DIRS
CORNERS = [d for d in DIRS if d[0] and d[1]]
BESIDE = [d for d in ALL if d not in CORNERS]
FAR = [(dx, dy) for dx in (-2, 2) for dy in (-1, 0, 1)]
XE0, YE0, H0 = 16, 24, 4
XE1, YE1, H1 = 14, 18, 5
L0, L1 = 384, 256
R0, R1, R2, R3 = 144, 80, 96, 48


def up128(n):
    return -(-n // 128) * 128


def lane0(x, y):
    return (y + H0) * XE0 + x + H0


def lane1(x, y):
    return (y + H1) * XE1 + x + H1


def tables(nx, ny, nz):
    x2, y2 = 2 * nx, 4 * ny
    l2, l3 = up128(x2 * y2), up128(nx * 2 * ny)
    t = {}
    place0 = np.zeros((384, L0), np.float32)
    sel0 = np.zeros((32, L0), np.float32)
    unsel = np.zeros((128, L0), np.float32)
    for x in range(8):
        for y in range(16):
            place0[x * 16 + y, lane0(x, y)] = 1
            unsel[x * 16 + y, lane0(x, y)] = 1
            sel0[(x // 2) * 8 + y // 2, lane0(x, y)] = 0.125
    for x in range(8):
        for y in range(16):
            place0[128 + x * 16 + y, lane0(x + 8 if x < 4 else x - 8, y)] = 1
        for yi in range(H0):
            place0[256 + x * 4 + yi, lane0(x, yi - H0)] = 1
            place0[288 + x * 4 + yi, lane0(x, yi + 16)] = 1
            if x >= 4:
                place0[320 + (x - 4) * 4 + yi, lane0(x - 8, yi - H0)] = 1
                place0[336 + (x - 4) * 4 + yi, lane0(x - 8, yi + 16)] = 1
            else:
                place0[352 + x * 4 + yi, lane0(x + 8, yi - H0)] = 1
                place0[368 + x * 4 + yi, lane0(x + 8, yi + 16)] = 1
    place1 = np.zeros((384, L1), np.float32)
    for d, (sx, sy) in enumerate([(0, 0)] + DIRS):
        for x in range(4):
            for y in range(8):
                xx, yy = x + 4 * sx, y + 8 * sy
                if -H1 <= xx < 4 + H1 and -H1 <= yy < 8 + H1:
                    place1[32 * d + x * 8 + y, lane1(xx, yy)] = 1
    for e, (sx, sy) in enumerate(FAR):
        for y in range(8):
            xx, yy = (-5 if sx < 0 else 8), y + 8 * sy
            if -H1 <= yy < 8 + H1:
                place1[288 + 8 * e + y, lane1(xx, yy)] = 1
    sel1 = np.zeros((8, L1), np.float32)
    quarter = np.zeros((8, L1), np.float32)
    for x in range(4):
        for y in range(8):
            sel1[x // 2, lane1(x, y)] = 0.125
            quarter[y // 2, lane1(x, y)] = 1
    prol0 = np.zeros((L1, L0), np.float32)
    for x in range(-H0, 8 + H0):
        for y in range(-H0, 16 + H0):
            prol0[lane1(x // 2, y // 2), lane0(x, y)] = 1
    perm2 = np.zeros((nx * ny * 8, l2), np.float32)
    for a in range(nx):
        for b in range(ny):
            for i in range(2):
                for j in range(4):
                    perm2[j * nx * ny * 2 + (a * ny + b) * 2 + i, (b * 4 + j) * x2 + a * 2 + i] = 1
    rest2 = np.zeros((l2, l3), np.float32)
    for x in range(x2):
        for y in range(y2):
            rest2[y * x2 + x, (y // 2) * nx + x // 2] = 0.125
    prol2 = (rest2.T != 0).astype(np.float32)
    kx1 = np.zeros((32, 128), np.float32)
    kx2 = np.zeros((4, 8, 128), np.float32)
    for x in range(8):
        for y in range(16):
            kx1[(x // 2) * 8 + y // 2, x * 16 + y] = 0.25
            kx2[y // 4, x // 4, x * 16 + y] = 0.0625
    kz1 = np.zeros((128, 128), np.float32)
    kz2 = np.zeros((128, 128), np.float32)
    for z in range(128):
        kz1[z, z // 2] = 0.5
        for c in range(4):
            kz2[z, 32 * c + z // 4] = 0.25
    coord = np.full((16, max(L0, l2)), OUT, np.int32)
    for x in range(-H0, 8 + H0):
        for y in range(-H0, 16 + H0):
            coord[0:2, lane0(x, y)] = x, y
    for x in range(-H1, 4 + H1):
        for y in range(-H1, 8 + H1):
            coord[2:4, lane1(x, y)] = x, y
            coord[8, lane1(x, y)] = (y // 2) * x2 + x // 2
    for x in range(x2):
        for y in range(y2):
            coord[4:6, y * x2 + x] = x, y
    for x in range(nx):
        for y in range(2 * ny):
            coord[6:8, y * nx + x] = x, y
            coord[9, y * nx + x] = (x % 2) * ny * nz + (y // 2) * nz
    coord[10:14, 0:L1] = quarter[0:4]
    k = np.arange(nx * ny * 8)
    coord[14, 0:len(k)] = k // 2 % ny
    sel0r = np.concatenate([sel0] * 4, axis=0).T
    names = dict(sel0r=sel0r, place0=place0, sel0=sel0, unsel=unsel, place1=place1, sel1=sel1, prol0=prol0, perm2=perm2, rest2=rest2,
                 prol2=prol2, kx1=kx1, kx2=kx2.reshape(32, 128), kz1=kz1, kz2=kz2)
    t = {k: v.astype(jnp.bfloat16) for k, v in names.items()}
    t["coord"] = coord
    return t


def split(x):
    hi = x.astype(BF16)
    return hi, (x - hi.astype(F32)).astype(BF16)


def times(x, w):
    rows = x.shape[0]
    both = jnp.dot(jnp.concatenate(split(x), axis=0), w, preferred_element_type=F32)
    return both[:rows] + both[rows:]


def select_t(w, x):
    dims = (((1,), (1,)), ((), ()))
    hi, lo = split(x)
    return lax.dot_general(w, hi, dims, preferred_element_type=F32) + lax.dot_general(w, lo, dims, preferred_element_type=F32)


def left(w, x):
    hi, lo = split(x)
    return jnp.dot(w, hi, preferred_element_type=F32) + jnp.dot(w, lo, preferred_element_type=F32)


def build(nx, ny, nz):
    x2, y2 = 2 * nx, 4 * ny
    l2, l3 = up128(x2 * y2), up128(nx * 2 * ny)
    consts = tables(nx, ny, nz)
    names = list(consts)

    n_sem = 19

    scratch = dict(
        x0=pltpu.VMEM((3, 8, 16, 128), F32),
        pack0=pltpu.VMEM((3, 8, 8, 128), F32),
        y0=pltpu.VMEM((3, 16, 8, 128), F32),
        slab0=pltpu.VMEM((3, 2, 2, 8, 128), F32),
        slabs0=pltpu.VMEM((3, 2, 9, 8, 128), F32),
        rhs0=pltpu.VMEM((R0, L0), F32),
        nat1=pltpu.VMEM((3, 48, 8, 128), F32),
        slab1=pltpu.VMEM((3, 2, 8, 128), F32),
        slabs1=pltpu.VMEM((3, 2, 9, 8, 128), F32),
        ext1=pltpu.VMEM((R1, L1), F32),
        yz2=pltpu.VMEM((3, 3, ny + 8, 2, 128), F32),
        xs2=pltpu.VMEM((3, nx, 3, ny + 8, 2, 128), F32),
        cells=pltpu.VMEM((3, 8, 16, 128), F32),
        m0=pltpu.VMEM((6, R0, L0), F32),
        c0=pltpu.VMEM((3, R0, L0), F32),
        m1=pltpu.VMEM((6, R1, L1), F32),
        c1=pltpu.VMEM((3, R1, L1), F32),
        m2=pltpu.VMEM((6, R2, l2), F32),
        c2=pltpu.VMEM((3, R2, l2), F32),
        v0=pltpu.VMEM((2, L0 // 128, R0 + 16, 128), F32),
        v1=pltpu.VMEM((2, L1 // 128, R1 + 16, 128), F32),
        v2=pltpu.VMEM((2, l2 // 128, R2 + 16, 128), F32),
        m3=pltpu.VMEM((6, R3, l3), F32),
        c3=pltpu.VMEM((2, R3, l3), F32),
        pairs=pltpu.VMEM((max(L0, l2) // 128, 160, 128), F32),
        agg=pltpu.VMEM((nx // 2, 2 * ny * nz), jnp.int32),
        prol1=pltpu.VMEM((l2, L1), BF16),
        zero16=pltpu.VMEM((2, 4, 16, 128), F32),
        zero8=pltpu.VMEM((2, 4, 8, 128), F32),
        zero2=pltpu.VMEM((2, 128), F32),
        zero_w=pltpu.VMEM((8, L1), F32),
        void8=pltpu.VMEM((104, 8, 128), F32),
        void2=pltpu.VMEM((max(nx * 3 * ny, nx * 15, 16), 2, 128), F32),
        lsem=pltpu.SemaphoreType.DMA((4,)),
        ssem=pltpu.SemaphoreType.DMA((n_sem,)),
        rsem=pltpu.SemaphoreType.DMA((n_sem,)),
    )
    keys = list(scratch)
    held = [pltpu.VMEM(consts[k].shape, consts[k].dtype) for k in names]

    def kernel(rhs_hbm, coef_hbm, agg_hbm, *rest):
        out = rest[len(names)]
        s = dict(zip(keys, rest[len(names) + 1:]))
        local = dict(zip(names, rest[len(names) + 1 + len(keys):]))
        rhs, coef = s["cells"].at[0], s["cells"].at[1]
        early = ["kx1", "kx2", "kz1", "kz2", "coord"]
        late = [k for k in names if k not in early]
        sources = dict(zip(names, rest))
        loads = {"rhs": [(rhs_hbm, rhs)], "coef": [(coef_hbm, coef)],
                 "early": [(sources[k], local[k]) for k in early] + [(agg_hbm, s["agg"])], "late": [(sources[k], local[k]) for k in late]}
        loads = {k: [pltpu.make_async_copy(a, b, s["lsem"].at[i]) for a, b in pairs] for i, (k, pairs) in enumerate(loads.items())}
        waited = set()

        def ready(k):
            if k not in waited:
                waited.add(k)
                for load in loads[k]:
                    load.wait()

        class Table:
            def __getitem__(self, k):
                ready("early" if k in early else "late")
                return local[k]

        c = Table()
        gx, gy, gz = lax.axis_index("gx"), lax.axis_index("gy"), lax.axis_index("gz")

        def has(dx, dy, dz):
            ok = None
            for g, d, n in ((gx, dx, nx), (gy, dy, ny), (gz, dz, nz)):
                if d:
                    here = (g + d >= 0) if d < 0 else (g + d < n)
                    ok = here if ok is None else ok & here
            return ok

        for k in ("coef", "rhs"):
            loads[k][0].start()
        stages = [0]
        absent = {}

        class Copy:
            def __init__(self, src, dst, there, send_if):
                i = stages[0]
                self.make = lambda: pltpu.make_async_remote_copy(
                    src_ref=src, dst_ref=dst, send_sem=s["ssem"].at[i], recv_sem=s["rsem"].at[i],
                    device_id=there, device_id_type=MESH)
                self.send_if = send_if
                self.hops = 0

            def under(self, f):
                if self.send_if is None:
                    f()
                else:
                    pl.when(self.send_if)(f)

            def start(self):
                self.under(lambda: self.make().start())

            def sent(self):
                self.under(lambda: self.make().wait_send())

        def toward(dx, dy, dz, src, dst, zero):
            i = stages[0]
            absent.setdefault((-dx, -dy, -dz), []).append(lambda: pltpu.make_async_copy(zero, dst, s["rsem"].at[i]).start())
            copy = Copy(src, dst, (gx + dx, gy + dy, gz + dz), has(dx, dy, dz))
            copy.hops = abs(dx) + abs(dy) + abs(dz)
            return copy

        class Stage:
            def __init__(self, make, void, size):
                self.copies = sorted(make(), key=lambda copy: -copy.hops)
                self.i, self.void, self.size = stages[0], void, size
                stages[0] += 1

            def start(self):
                for copy in self.copies:
                    copy.start()

            def drain(self):
                for copy in self.copies:
                    copy.sent()

            def arrive(self):
                all_of_it = self.void.at[0:self.size]
                pltpu.make_async_copy(all_of_it, all_of_it, s["rsem"].at[self.i]).wait()

        def halo0(n):
            fields = 2 if n.start == 0 else 1
            copies = []
            for dx, dy in DIRS:
                if dy == 0:
                    xs = slice(4, 8) if dx > 0 else slice(0, 4)
                    copies.append(toward(dx, dy, 0, s["cells"].at[n, xs], s["x0"].at[n, xs], s["zero16"].at[0:fields]))
                    continue
                face = 0 if dy > 0 else 4
                if dx == 0:
                    mine, to = slice(face, face + 4), slice(face, face + 4)
                else:
                    mine = slice(face + 2, face + 4) if dx > 0 else slice(face, face + 2)
                    first = (8 if dx > 0 else 12) + (0 if dy > 0 else 2)
                    to = slice(first, first + 2)
                copies.append(toward(dx, dy, 0, s["pack0"].at[n, mine], s["y0"].at[n, to], s["zero8"].at[0:fields, 0:to.stop - to.start]))
            return copies

        def slab_halo(slab, slabs, zero, planes=ALL):
            return [toward(dx, dy, dz, slab(0 if dz < 0 else 1, dy), slabs(1 if dz < 0 else 0, ALL.index((-dx, -dy))), zero)
                    for dx, dy in planes for dz in (-1, 1)]

        def plane1(n):
            copies = []
            for dx, dy in DIRS:
                d = ALL.index((-dx, -dy))
                copies.append(toward(dx, dy, 0, s["nat1"].at[n, 0:4], s["nat1"].at[n, 4 * d:4 * d + 4], s["zero8"].at[0]))
            return copies

        def far1(n):
            copies = []
            for dx, dy in FAR:
                e = FAR.index((-dx, -dy))
                i = 3 if dx > 0 else 0
                copies.append(toward(dx, dy, 0, s["nat1"].at[n, i:i + 1], s["nat1"].at[n, 36 + e:37 + e], s["zero8"].at[0, 0:1]))
            return copies

        def z_halo1():
            return [toward(0, 0, -1, s["ext1"].at[8:16, :], s["ext1"].at[R1 - 8:R1, :], s["zero_w"]),
                    toward(0, 0, 1, s["ext1"].at[R1 - 16:R1 - 8, :], s["ext1"].at[0:8, :], s["zero_w"])]

        def yzline():
            mine = s["yz2"].at[0, 1, gy + 4]
            copies = []
            for d in sorted(range(ny), key=lambda d: -min(d, ny - d)):
                for dz in (-1, 1, 0):
                    if d or dz:
                        copies.append(Copy(mine, s["yz2"].at[0, 1 - dz, gy + 4], (gx, lax.rem(gy + d, ny), gz + dz), has(0, 0, dz)))
            i = stages[0]
            for dz in (-1, 1):
                for d in range(ny):
                    absent.setdefault((0, 0, dz), []).append(
                        lambda dz=dz, d=d: pltpu.make_async_copy(s["zero2"], s["yz2"].at[0, 1 + dz, 4 + d], s["rsem"].at[i]).start())
            return copies

        def yzwindow(n, offsets):
            copies = []
            i = stages[0]
            for dy in offsets:
                for dz in (-1, 1, 0):
                    if dy or dz:
                        copy = Copy(s["yz2"].at[n, 1, gy + 4], s["yz2"].at[n, 1 - dz, gy + 4], (gx, gy + dy, gz + dz), has(0, dy, dz))
                        copy.hops = abs(dy) + abs(dz)
                        copies.append(copy)
                        absent.setdefault((0, dy, dz), []).append(
                            lambda dy=dy, dz=dz: pltpu.make_async_copy(s["zero2"], s["yz2"].at[n, 1 + dz, gy + dy + 4], s["rsem"].at[i]).start())
            return copies

        def xline(n, windows):
            copies = []
            for d in sorted(range(1, nx), key=lambda d: -min(d, nx - d)):
                for first, size in windows:
                    at = pl.ds(first, size)
                    copies.append(Copy(s["yz2"].at[n, :, at], s["xs2"].at[n, gx, :, at], (lax.rem(gx + d, nx), gy, gz), None))
            return copies

        E0, E1, C1, Y2, X2, YF, XF = {}, [], [None], [], [], [None], [None]
        for first, fields in ((0, 2), (2, 1)):
            n = slice(first, first + fields)
            E0[first] = Stage(lambda: halo0(n) + slab_halo(lambda side, dy: s["slab0"].at[n, side, 1 if dy else 0],
                                                           lambda side, d: s["slabs0"].at[n, side, d], s["zero8"].at[0:fields, 0]),
                              s["void8"], 50 * fields)
        for n in range(3):
            if n:
                ends = (lambda side, dy: s["slab1"].at[n, side], lambda side, d: s["slabs1"].at[n, side, d], s["zero8"].at[0, 0])
                E1.append(Stage(lambda: slab_halo(*ends, BESIDE) + plane1(n), s["void8"], 42))
                C1.append(Stage(lambda: slab_halo(*ends, CORNERS), s["void8"], 8))
            else:
                E1.append(Stage(lambda: plane1(0) + far1(0), s["void8"], 38))
            if n:
                YF.append(Stage(lambda: yzwindow(n, (-4, -3, 3, 4)), s["void2"], 12))
                Y2.append(Stage(lambda: yzwindow(n, (-2, -1, 0, 1, 2)), s["void2"], 14))
                X2.append(Stage(lambda: xline(n, [(gy + 2, 5)]), s["void2"], (nx - 1) * 15))
                XF.append(Stage(lambda: xline(n, [(gy, 2), (gy + 7, 2)]), s["void2"], (nx - 1) * 12))
            else:
                Y2.append(Stage(yzline, s["void2"], 3 * ny - 1))
                X2.append(Stage(lambda: xline(0, [(4, ny)]), s["void2"], (nx - 1) * 3 * ny))
        Z1 = Stage(z_halo1, s["void8"], 4)

        for k in ("zero16", "zero8", "zero2", "zero_w"):
            s[k][...] = jnp.zeros(s[k].shape, F32)

        barrier = pltpu.get_barrier_semaphore()
        total = jnp.int32(nx - 1 + ny - 1)
        by_distance = sorted(range(ny), key=lambda d: -min(d, ny - d))
        for dz in (-1, 1):
            ok = has(0, 0, dz)
            total = total + ny * ok.astype(jnp.int32)

            @pl.when(ok)
            def _(dz=dz):
                for d in by_distance:
                    pl.semaphore_signal(barrier, inc=1, device_id=(gx, lax.rem(gy + d, ny), gz + dz), device_id_type=MESH)
        for d in by_distance[:-1]:
            pl.semaphore_signal(barrier, inc=1, device_id=(gx, lax.rem(gy + d, ny), gz), device_id_type=MESH)
        for d in range(1, nx):
            pl.semaphore_signal(barrier, inc=1, device_id=(lax.rem(gx + d, nx), gy, gz), device_id_type=MESH)
        near = [(dx, dy, 0) for dx, dy in DIRS + FAR if dx and dy] + [(dx, dy, dz) for dx, dy in DIRS if dx for dz in (-1, 1)]
        for dx, dy, dz in near:
            ok = has(dx, dy, dz)
            total = total + ok.astype(jnp.int32)

            @pl.when(ok)
            def _(dx=dx, dy=dy, dz=dz):
                pl.semaphore_signal(barrier, inc=1, device_id=(gx + dx, gy + dy, gz + dz), device_id_type=MESH)

        for k in ("early", "late"):
            for load in loads[k]:
                load.start()

        for k in ("v0", "v1", "v2"):
            rows = s[k].shape[2]
            for b in range(2):
                for j in range(s[k].shape[1]):
                    s[k][b, j, 0:8] = jnp.zeros((8, 128), F32)
                    s[k][b, j, rows - 8:rows] = jnp.zeros((8, 128), F32)
        s["nat1"][0, 42:48] = jnp.zeros((6, 8, 128), F32)
        for n in (1, 2):
            s["nat1"][n, 36:48] = jnp.zeros((12, 8, 128), F32)

        def post0(n, nat, flipped):
            cells = nat.reshape(8, 16, 128)
            high, low = cells[:, 12:16].reshape(32, 128), cells[:, 0:4].reshape(32, 128)
            s["pack0"][n, 0:4] = high.reshape(4, 8, 128)
            s["pack0"][n, 4:8] = low.reshape(4, 8, 128)
            faces = jnp.concatenate([high, low, high[16:32], low[16:32], high[0:16], low[0:16]], axis=0).T
            for kind, rows in enumerate((flipped, faces)):
                s["slab0"][n, 0, kind] = rows[0:8]
                s["slab0"][n, 1, kind] = rows[120:128]

        lane = lax.broadcasted_iota(jnp.int32, (8, 128), 1)

        def by_quarter(parts):
            return jnp.where(lane < 32, parts[0], jnp.where(lane < 64, parts[1], jnp.where(lane < 96, parts[2], parts[3])))

        ready("coef")
        k_nat = coef[...].reshape(128, 128)
        k_flip = k_nat.T
        post0(1, k_nat, k_flip)
        ready("rhs")
        f_nat = rhs[...].reshape(128, 128)
        f_flip = f_nat.T
        post0(0, f_nat, f_flip)
        pl.semaphore_wait(barrier, total)
        E0[0].start()
        for place, fills in absent.items():
            @pl.when(jnp.logical_not(has(*place)))
            def _(fills=fills):
                for fill in fills:
                    fill()

        k1 = times(left(c["kx1"][...], k_nat), c["kz1"][...])
        s["nat1"][0, 0:4] = k1.reshape(4, 8, 128)
        E1[0].start()
        k2_parts = times(left(c["kx2"][...], k_nat), c["kz2"][...])
        s["yz2"][0, 1, gy + 4] = by_quarter([k2_parts[8 * q:8 * q + 8] for q in range(4)])[0:2]
        Y2[0].start()

        def shifts(v, xe):
            rows, lanes = v.shape
            tiles = [v[:, i:i + 128] for i in range(0, lanes, 128)]
            if 128 % xe or len(tiles) == 1:
                beside = (pltpu.roll(v, lanes - 1, 1), pltpu.roll(v, 1, 1))
            else:
                beside = tuple(jnp.concatenate([pltpu.roll(tile, d, 1) for tile in tiles], axis=1) for d in (127, 1))
            return beside + (pltpu.roll(v, lanes - xe, 1), pltpu.roll(v, xe, 1),
                    pltpu.roll(v, rows - 1, 0), pltpu.roll(v, 1, 0))

        def setup(k, xe, factor, inside, inner, extra, m, consts_ref):
            rows, lanes = k.shape
            ws = []
            for i, other in enumerate(shifts(k, xe)):
                if inner is not None and i < 4:
                    other = jnp.where(inner[i], other, 0.0)
                ws.append(0.5 * (k + other))
            diag = ws[0]
            for w in ws[1:]:
                diag = diag + w
            diag = factor * diag
            minv = jnp.where(inside, 0.8 / diag, 0.0)
            for i, w in enumerate(ws):
                link = (factor * minv) * w
                if inner is not None and i < 4:
                    link = jnp.where(inner[i], link, 0.0)
                if extra is not None:
                    link = jnp.where(extra[i], link, 0.0)
                m[i] = link
            consts_ref[0] = minv
            if consts_ref.shape[0] > 2:
                consts_ref[1] = 1.25 * diag

        def sweep(v, g, m, xe, first=0):
            total = 0.2 * v + g
            for i, other in enumerate(shifts(v, xe)):
                total = total + m[i, first:first + v.shape[0]] * other
            return total

        def put(vs, k, value, first=0):
            for j in range(vs.shape[1]):
                vs[k, j, 8 + first:8 + first + value.shape[0]] = value[:, 128 * j:128 * j + 128]

        def get(vs, k, rows, first=0):
            parts = [vs[k, j, 8 + first:8 + first + rows] for j in range(vs.shape[1])]
            return parts[0] if len(parts) == 1 else jnp.concatenate(parts, axis=1)

        def sweep_in(vs, a, b, g, m, xe, rows, first=0):
            count = vs.shape[1]

            def body(i, carry):
                row = first + 8 * i
                at = pl.ds(pl.multiple_of(row, 8), 8)
                centre = [vs[a, j, pl.ds(row + 8, 8), :] for j in range(count)]
                right, left_, above, below = ([pltpu.roll(v, d, 1) for v in centre] for d in (127, 1, 128 - xe, xe))
                for j in range(count):
                    after, before = (j + 1) % count, (j - 1) % count
                    lanes = slice(128 * j, 128 * j + 128)
                    xr, xl, yr, yl = right[j], left_[j], above[j], below[j]
                    if count > 1:
                        if 128 % xe:
                            xr = jnp.where(lane < 127, xr, right[after])
                            xl = jnp.where(lane > 0, xl, left_[before])
                        yr = jnp.where(lane < 128 - xe, yr, above[after])
                        yl = jnp.where(lane >= xe, yl, below[before])
                    total = 0.2 * centre[j] + g[at, lanes]
                    others = (xr, xl, yr, yl, vs[a, j, pl.ds(row + 9, 8), :], vs[a, j, pl.ds(row + 7, 8), :])
                    for q, other in enumerate(others):
                        total = total + m[q, at, lanes] * other
                    vs[b, j, pl.ds(row + 8, 8), :] = total
                return carry

            lax.fori_loop(0, rows // 8, body, 0, unroll=True)

        def coords(level, lanes, rows, x_off, y_off, z_off):
            x = c["coord"][2 * level:2 * level + 1, 0:lanes] + x_off
            y = c["coord"][2 * level + 1:2 * level + 2, 0:lanes] + y_off
            z = lax.broadcasted_iota(jnp.int32, (rows, lanes), 0) + z_off
            return x, y, z

        def inside_of(x, y, z, sizes):
            plane = (x >= 0) & (x < sizes[0]) & (y >= 0) & (y < sizes[1])
            return jnp.broadcast_to(plane, z.shape) & (z >= 0) & (z < sizes[2])

        def assemble0(n, flipped):
            blocks = [flipped, s["x0"][n].reshape(128, 128).T, s["y0"][n].reshape(128, 128).T]
            ends = []
            for side in range(2):
                def at(dx, dy, side=side):
                    return s["slabs0"][n, side, ALL.index((dx, dy))]

                diagonals = jnp.where(lane < 80, at(-1, -1), jnp.where(lane < 96, at(-1, 1), jnp.where(lane < 112, at(1, -1), at(1, 1))))
                ends.append(jnp.concatenate([
                    at(0, 0), jnp.where(lane < 64, at(1, 0), at(-1, 0)),
                    jnp.where(lane < 32, at(0, -1), jnp.where(lane < 64, at(0, 1), diagonals))], axis=1))
            wide = jnp.concatenate([ends[0], jnp.concatenate(blocks, axis=1), ends[1]], axis=0)
            return times(wide, c["place0"][...])

        def natural1(n):
            nat = s["nat1"][n].reshape(384, 128)
            return jnp.concatenate([nat[128 * i:128 * i + 128].T for i in range(3)], axis=1)[0:64]

        def slabs_of(n, side, planes):
            slabs = [s["slabs1"][n, side, d] if ALL[d] in planes else jnp.zeros((8, 128), F32) for d in range(9)]
            return jnp.concatenate([by_quarter(slabs[0:4]), by_quarter(slabs[4:8]), jnp.where(lane < 32, slabs[8], 0.0)], axis=1)

        def assemble1(n):
            ends = [slabs_of(n, side, BESIDE) for side in range(2)]
            wide = jnp.concatenate([ends[0], natural1(n), ends[1]], axis=0)
            return times(wide, c["place1"][...])

        def corners1(n):
            C1[n].arrive()
            more = times(jnp.concatenate([slabs_of(n, side, CORNERS) for side in range(2)], axis=0), c["place1"][...])
            for rows, part in ((slice(0, 8), more[0:8]), (slice(R1 - 8, R1), more[8:16])):
                s["c1"][2, rows] = s["c1"][2, rows] + s["c1"][0, rows] * part
            presmooth(s["v1"], s["m1"], s["c1"], XE1)

        def drain(*done):
            for stage in done:
                stage.drain()

        def gather2_x(n):
            Y2[n].arrive()
            X2[n].start()
            if n:
                YF[n].arrive()
                XF[n].start()
            s["xs2"][n, gx] = s["yz2"][n]

        def gather2(n):
            X2[n].arrive()
            if n:
                XF[n].arrive()
            rows = []
            for dz in range(3):
                flipped = s["xs2"][n, :, dz, 4:4 + ny].reshape(nx * ny * 2, 128).T
                rows.append(jnp.concatenate([flipped[32 * q:32 * q + 32] for q in range(4)], axis=1))
            wide = jnp.concatenate(rows, axis=0)
            if n:
                device = c["coord"][14:15, 0:wide.shape[1]] - gy
                wide = jnp.where((device >= -4) & (device <= 4), wide, 0.0)
            return times(wide, c["perm2"][...])

        x1, y1, z1 = coords(1, L1, R1, 4 * gx, 8 * gy, 64 * gz - 8)
        target = c["coord"][8:9, 0:L1] + (2 * gx + 4 * gy * x2)
        target = jnp.where((x1 >= 0) & (x1 < 4 * nx) & (y1 >= 0) & (y1 < 8 * ny), target, -1)
        s["prol1"][...] = jnp.where(lax.broadcasted_iota(jnp.int32, (l2, L1), 0) == target, 1.0, 0.0).astype(BF16)

        near_owner = []
        xb = c["coord"][6:7, 0:l3]
        for i in (jnp.maximum(gz - 1, 0), gz, jnp.minimum(gz + 1, nz - 1)):
            pick = lax.broadcasted_iota(jnp.int32, (2 * ny * nz, l3), 0) == c["coord"][9:10, 0:l3] + i
            picked = jnp.dot(s["agg"][...].astype(F32).astype(BF16), jnp.where(pick, 1.0, 0.0).astype(BF16), preferred_element_type=F32)
            mine = jnp.zeros((1, l3), F32)
            for r in range(nx // 2):
                mine = jnp.where(xb // 2 == r, picked[r:r + 1], mine)
            near_owner.append(jnp.broadcast_to(mine, (16, l3)))
        owner = jnp.concatenate(near_owner, axis=0)

        E0[0].arrive()
        k0 = assemble0(1, k_flip)
        x0, y0, z0 = coords(0, L0, R0, 8 * gx, 16 * gy, 128 * gz - 8)
        setup(k0, XE0, 1.0, inside_of(x0, y0, z0, (8 * nx, 16 * ny, 128 * nz)), None, None, s["m0"], s["c0"])
        f0 = assemble0(0, f_flip)
        s["rhs0"][...] = f0
        s["c0"][2] = s["c0"][0] * f0

        def halved(v, first, half):
            rows, lanes = v.shape
            sums = []
            for j in range(lanes // 128):
                s["pairs"][j, 0:rows] = v[:, 128 * j:128 * j + 128]
                sums.append(s["pairs"][j, pl.ds(first, half, stride=2), :] + s["pairs"][j, pl.ds(first + 1, half, stride=2), :])
            return sums[0] if len(sums) == 1 else jnp.concatenate(sums, axis=1)

        def doubled(v, first, rows):
            half, lanes = v.shape
            parts = []
            for j in range(lanes // 128):
                part = v[:, 128 * j:128 * j + 128]
                s["pairs"][j, pl.ds(0, half, stride=2), :] = part
                s["pairs"][j, pl.ds(1, half, stride=2), :] = part
                parts.append(s["pairs"][j, first:first + rows])
            return parts[0] if len(parts) == 1 else jnp.concatenate(parts, axis=1)

        def presmooth(vs, m, consts_ref, xe):
            put(vs, 0, consts_ref[2])
            sweep_in(vs, 0, 1, consts_ref.at[2], m, xe, m.shape[1])

        def down(vs, m, consts_ref, xe):
            rows = m.shape[1]
            presmooth(vs, m, consts_ref, xe)
            sweep_in(vs, 1, 0, consts_ref.at[2], m, xe, rows)
            return consts_ref[1] * (get(vs, 0, rows) - get(vs, 1, rows))

        def up(vs, m, consts_ref, xe, correction, first=0):
            rows = correction.shape[0]
            put(vs, 0, get(vs, 1, rows, first) + correction, first)
            sweep_in(vs, 0, 1, consts_ref.at[2], m, xe, rows, first)
            sweep_in(vs, 1, 0, consts_ref.at[2], m, xe, rows, first)
            return get(vs, 0, rows, first)

        E1[0].arrive()
        s["ext1"][8:R1 - 8] = times(natural1(0), c["place1"][...])
        Z1.start()

        for cycle in range(2):
            n = 1 + cycle
            r = down(s["v0"], s["m0"], s["c0"], XE0)
            half = halved(r, 8, 64)
            ends = times(jnp.concatenate([half[0:8], half[56:64]], axis=0), c["sel0r"][...])
            s["slab1"][n] = ends.reshape(2, 8, 128)
            s["nat1"][n, 0:4, :, 0:64] = select_t(c["sel0"][...], half).reshape(4, 8, 64)
            E1[n].start()
            C1[n].start()
            if cycle == 0:
                gather2_x(0)
                Z1.arrive()
                inside = inside_of(x1, y1, z1, (4 * nx, 8 * ny, 64 * nz))
                setup(s["ext1"][...], XE1, 0.25, inside, None, None, s["m1"], s["c1"])
            if cycle == 1:
                drain(X2[1], XF[1])
            E1[n].arrive()
            s["c1"][2] = s["c1"][0] * assemble1(n)
            half = halved(down(s["v1"], s["m1"], s["c1"], XE1), 8, 32)
            quarters = [jnp.where(c["coord"][10 + q:11 + q, 0:L1] > 0, half, 0.0) for q in range(4)]
            s["yz2"][n, 1, gy + 4] = select_t(c["sel1"][...], jnp.concatenate(quarters, axis=0))[0:2]
            YF[n].start()
            Y2[n].start()
            if cycle == 0:
                k2 = gather2(0)
                x, y, z = coords(2, l2, R2, 0, 0, 32 * gz - 32)
                inner = [jnp.broadcast_to(q, z.shape) for q in (x + 1 < x2, x > 0, y + 1 < y2, y > 0)]
                setup(k2, x2, 0.0625, inside_of(x, y, z, (x2, y2, 32 * nz)), inner, None, s["m2"], s["c2"])
                k3 = times(halved(k2, 0, R3), c["rest2"][...])
                x, y, z = coords(3, l3, R3, 0, 0, 16 * gz - 16)
                inner = [jnp.broadcast_to(q, z.shape) for q in (x + 1 < nx, x > 0, y + 1 < 2 * ny, y > 0)]
                same = [other == owner for other in shifts(owner, nx)]
                setup(k3, nx, 0.015625, inside_of(x, y, z, (nx, 2 * ny, 16 * nz)), inner, same, s["m3"], s["c3"])
            if cycle == 0:
                drain(E0[0], E1[0], Y2[0], Z1)
            else:
                drain(E0[2])
            corners1(n)
            gather2_x(n)
            if cycle == 0:
                drain(E1[1], C1[1], X2[0])
            else:
                drain(E1[2], C1[2], Y2[2], YF[2])
            f2 = gather2(n)
            s["c2"][2] = s["c2"][0] * f2
            r = down(s["v2"], s["m2"], s["c2"], x2)
            g3 = s["c3"][0] * times(halved(r, 0, R3), c["rest2"][...])
            e = g3
            for j in range(COARSE_SWEEPS - 1):
                e = sweep(e, g3, s["m3"], nx)
            v = up(s["v2"], s["m2"], s["c2"], x2, doubled(times(e[8:40], c["prol2"][...]), 8, 48), 24)
            fine = times(v, s["prol1"][...])
            v = up(s["v1"], s["m1"], s["c1"], XE1, doubled(fine, 8, R1))
            fine = times(v, c["prol0"][...])
            v = up(s["v0"], s["m0"], s["c0"], XE0, doubled(fine, 8, R0))
            nat = select_t(c["unsel"][...], v[8:R0 - 8])
            if cycle == 0:
                s["cells"][2] = nat.reshape(8, 16, 128)
                flipped = nat.T
                post0(2, nat, flipped)
                E0[2].start()
                drain(Y2[1], YF[1])
                E0[2].arrive()
                now = assemble0(2, flipped)
                put(s["v0"], 0, now)
                s["c0"][2] = s["c0"][0] * s["rhs0"][...]
                sweep_in(s["v0"], 0, 1, s["c0"].at[2], s["m0"], XE0, R0)
                s["c0"][2] = get(s["v0"], 1, R0) - get(s["v0"], 0, R0)
            else:
                out[...] = s["cells"][2] + nat.reshape(8, 16, 128)
        for k in loads:
            ready(k)
        drain(X2[2], XF[2])

    vmem = pl.BlockSpec(memory_space=pltpu.VMEM)
    hbm = pl.BlockSpec(memory_space=pl.ANY)

    def body(rhs, coef, agglom):
        agg = agglom.reshape(nx // 2, 2 * ny * nz)
        return pl.pallas_call(
            kernel,
            out_shape=pltpu.VMEM((8, 16, 128), F32),
            in_specs=[hbm, hbm, hbm] + [hbm] * len(names),
            out_specs=vmem,
            scratch_shapes=[scratch[k] for k in keys] + held,
            compiler_params=pltpu.CompilerParams(collective_id=0, has_side_effects=True, vmem_limit_bytes=60 * 1024 * 1024),
        )(rhs, coef, agg, *[jnp.asarray(consts[k]) for k in names])

    return body


def solution(mesh):
    body = build(mesh.shape["gx"], mesh.shape["gy"], mesh.shape["gz"])
    spec = P("gx", "gy", "gz")
    return jax.shard_map(body, mesh=mesh, in_specs=(spec, spec, P()), out_specs=spec, check_vma=False)
```

```python
import jax
import jax.numpy as jnp
import numpy as np
from jax import lax
from jax.experimental import pallas as pl
from jax.experimental.pallas import tpu as pltpu
from jax.sharding import PartitionSpec as P

F32 = jnp.float32
BF16 = jnp.bfloat16
MESH = pl.DeviceIdType.MESH
OUT = -100000
COARSE_SWEEPS = 8
DIRS = [(dx, dy) for dx in (-1, 0, 1) for dy in (-1, 0, 1) if (dx, dy) != (0, 0)]
ALL = [(0, 0)] + DIRS
CORNERS = [d for d in DIRS if d[0] and d[1]]
BESIDE = [d for d in ALL if d not in CORNERS]
FAR = [(dx, dy) for dx in (-2, 2) for dy in (-1, 0, 1)]
XE0, YE0, H0 = 16, 24, 4
XE1, YE1, H1 = 14, 18, 5
L0, L1 = 384, 256
R0, R1, R2, R3 = 144, 80, 96, 48


def up128(n):
    return -(-n // 128) * 128


def lane0(x, y):
    return (y + H0) * XE0 + x + H0


def lane1(x, y):
    return (y + H1) * XE1 + x + H1


def tables(nx, ny, nz):
    x2, y2 = 2 * nx, 4 * ny
    l2, l3 = up128(x2 * y2), up128(nx * 2 * ny)
    t = {}
    place0 = np.zeros((384, L0), np.float32)
    sel0 = np.zeros((32, L0), np.float32)
    unsel = np.zeros((128, L0), np.float32)
    for x in range(8):
        for y in range(16):
            place0[x * 16 + y, lane0(x, y)] = 1
            unsel[x * 16 + y, lane0(x, y)] = 1
            sel0[(x // 2) * 8 + y // 2, lane0(x, y)] = 0.125
    for x in range(8):
        for y in range(16):
            place0[128 + x * 16 + y, lane0(x + 8 if x < 4 else x - 8, y)] = 1
        for yi in range(H0):
            place0[256 + x * 4 + yi, lane0(x, yi - H0)] = 1
            place0[288 + x * 4 + yi, lane0(x, yi + 16)] = 1
            if x >= 4:
                place0[320 + (x - 4) * 4 + yi, lane0(x - 8, yi - H0)] = 1
                place0[336 + (x - 4) * 4 + yi, lane0(x - 8, yi + 16)] = 1
            else:
                place0[352 + x * 4 + yi, lane0(x + 8, yi - H0)] = 1
                place0[368 + x * 4 + yi, lane0(x + 8, yi + 16)] = 1
    place1 = np.zeros((384, L1), np.float32)
    for d, (sx, sy) in enumerate([(0, 0)] + DIRS):
        for x in range(4):
            for y in range(8):
                xx, yy = x + 4 * sx, y + 8 * sy
                if -H1 <= xx < 4 + H1 and -H1 <= yy < 8 + H1:
                    place1[32 * d + x * 8 + y, lane1(xx, yy)] = 1
    for e, (sx, sy) in enumerate(FAR):
        for y in range(8):
            xx, yy = (-5 if sx < 0 else 8), y + 8 * sy
            if -H1 <= yy < 8 + H1:
                place1[288 + 8 * e + y, lane1(xx, yy)] = 1
    sel1 = np.zeros((8, L1), np.float32)
    quarter = np.zeros((8, L1), np.float32)
    for x in range(4):
        for y in range(8):
            sel1[x // 2, lane1(x, y)] = 0.125
            quarter[y // 2, lane1(x, y)] = 1
    prol0 = np.zeros((L1, L0), np.float32)
    for x in range(-H0, 8 + H0):
        for y in range(-H0, 16 + H0):
            prol0[lane1(x // 2, y // 2), lane0(x, y)] = 1
    perm2 = np.zeros((nx * ny * 8, l2), np.float32)
    for a in range(nx):
        for b in range(ny):
            for i in range(2):
                for j in range(4):
                    perm2[j * nx * ny * 2 + (a * ny + b) * 2 + i, (b * 4 + j) * x2 + a * 2 + i] = 1
    rest2 = np.zeros((l2, l3), np.float32)
    for x in range(x2):
        for y in range(y2):
            rest2[y * x2 + x, (y // 2) * nx + x // 2] = 0.125
    prol2 = (rest2.T != 0).astype(np.float32)
    kx1 = np.zeros((32, 128), np.float32)
    kx2 = np.zeros((4, 8, 128), np.float32)
    for x in range(8):
        for y in range(16):
            kx1[(x // 2) * 8 + y // 2, x * 16 + y] = 0.25
            kx2[y // 4, x // 4, x * 16 + y] = 0.0625
    kz1 = np.zeros((128, 128), np.float32)
    kz2 = np.zeros((128, 128), np.float32)
    for z in range(128):
        kz1[z, z // 2] = 0.5
        for c in range(4):
            kz2[z, 32 * c + z // 4] = 0.25
    coord = np.full((16, max(L0, l2)), OUT, np.int32)
    for x in range(-H0, 8 + H0):
        for y in range(-H0, 16 + H0):
            coord[0:2, lane0(x, y)] = x, y
    for x in range(-H1, 4 + H1):
        for y in range(-H1, 8 + H1):
            coord[2:4, lane1(x, y)] = x, y
            coord[8, lane1(x, y)] = (y // 2) * x2 + x // 2
    for x in range(x2):
        for y in range(y2):
            coord[4:6, y * x2 + x] = x, y
    for x in range(nx):
        for y in range(2 * ny):
            coord[6:8, y * nx + x] = x, y
            coord[9, y * nx + x] = (x % 2) * ny * nz + (y // 2) * nz
    coord[10:14, 0:L1] = quarter[0:4]
    k = np.arange(nx * ny * 8)
    coord[14, 0:len(k)] = k // 2 % ny
    sel0r = np.concatenate([sel0] * 4, axis=0).T
    names = dict(sel0r=sel0r, place0=place0, sel0=sel0, unsel=unsel, place1=place1, sel1=sel1, prol0=prol0, perm2=perm2, rest2=rest2,
                 prol2=prol2, kx1=kx1, kx2=kx2.reshape(32, 128), kz1=kz1, kz2=kz2)
    t = {k: v.astype(jnp.bfloat16) for k, v in names.items()}
    t["coord"] = coord
    return t


def split(x):
    hi = x.astype(BF16)
    return hi, (x - hi.astype(F32)).astype(BF16)


def times(x, w):
    rows = x.shape[0]
    both = jnp.dot(jnp.concatenate(split(x), axis=0), w, preferred_element_type=F32)
    return both[:rows] + both[rows:]


def select_t(w, x):
    dims = (((1,), (1,)), ((), ()))
    hi, lo = split(x)
    return lax.dot_general(w, hi, dims, preferred_element_type=F32) + lax.dot_general(w, lo, dims, preferred_element_type=F32)


def left(w, x):
    hi, lo = split(x)
    return jnp.dot(w, hi, preferred_element_type=F32) + jnp.dot(w, lo, preferred_element_type=F32)


def build(nx, ny, nz):
    x2, y2 = 2 * nx, 4 * ny
    l2, l3 = up128(x2 * y2), up128(nx * 2 * ny)
    consts = tables(nx, ny, nz)
    names = list(consts)

    n_sem = 19

    scratch = dict(
        x0=pltpu.VMEM((3, 8, 16, 128), F32),
        pack0=pltpu.VMEM((3, 8, 8, 128), F32),
        y0=pltpu.VMEM((3, 16, 8, 128), F32),
        slab0=pltpu.VMEM((3, 2, 2, 8, 128), F32),
        slabs0=pltpu.VMEM((3, 2, 9, 8, 128), F32),
        rhs0=pltpu.VMEM((R0, L0), F32),
        nat1=pltpu.VMEM((3, 48, 8, 128), F32),
        slab1=pltpu.VMEM((3, 2, 8, 128), F32),
        slabs1=pltpu.VMEM((3, 2, 9, 8, 128), F32),
        ext1=pltpu.VMEM((R1, L1), F32),
        yz2=pltpu.VMEM((3, 3, ny + 8, 2, 128), F32),
        xs2=pltpu.VMEM((3, nx, 3, ny + 8, 2, 128), F32),
        cells=pltpu.VMEM((3, 8, 16, 128), F32),
        m0=pltpu.VMEM((6, R0, L0), F32),
        c0=pltpu.VMEM((3, R0, L0), F32),
        m1=pltpu.VMEM((6, R1, L1), F32),
        c1=pltpu.VMEM((3, R1, L1), F32),
        m2=pltpu.VMEM((6, R2, l2), F32),
        c2=pltpu.VMEM((3, R2, l2), F32),
        v0=pltpu.VMEM((2, L0 // 128, R0 + 16, 128), F32),
        v1=pltpu.VMEM((2, L1 // 128, R1 + 16, 128), F32),
        v2=pltpu.VMEM((2, l2 // 128, R2 + 16, 128), F32),
        m3=pltpu.VMEM((6, R3, l3), F32),
        c3=pltpu.VMEM((2, R3, l3), F32),
        pairs=pltpu.VMEM((max(L0, l2) // 128, 168, 128), F32),
        agg=pltpu.VMEM((nx // 2, 2 * ny * nz), jnp.int32),
        prol1=pltpu.VMEM((l2, L1), BF16),
        zero16=pltpu.VMEM((2, 4, 16, 128), F32),
        zero8=pltpu.VMEM((2, 4, 8, 128), F32),
        zero2=pltpu.VMEM((2, 128), F32),
        zero_w=pltpu.VMEM((8, L1), F32),
        void8=pltpu.VMEM((104, 8, 128), F32),
        void2=pltpu.VMEM((max(nx * 3 * ny, nx * 15, 16), 2, 128), F32),
        lsem=pltpu.SemaphoreType.DMA((4,)),
        ssem=pltpu.SemaphoreType.DMA((n_sem,)),
        rsem=pltpu.SemaphoreType.DMA((n_sem,)),
    )
    keys = list(scratch)
    held = [pltpu.VMEM(consts[k].shape, consts[k].dtype) for k in names]

    def kernel(rhs_hbm, coef_hbm, agg_hbm, *rest):
        out = rest[len(names)]
        s = dict(zip(keys, rest[len(names) + 1:]))
        local = dict(zip(names, rest[len(names) + 1 + len(keys):]))
        rhs, coef = s["cells"].at[0], s["cells"].at[1]
        early = ["kx1", "kx2", "kz1", "kz2", "coord"]
        late = [k for k in names if k not in early]
        sources = dict(zip(names, rest))
        loads = {"rhs": [(rhs_hbm, rhs)], "coef": [(coef_hbm, coef)],
                 "early": [(sources[k], local[k]) for k in early] + [(agg_hbm, s["agg"])], "late": [(sources[k], local[k]) for k in late]}
        loads = {k: [pltpu.make_async_copy(a, b, s["lsem"].at[i]) for a, b in pairs] for i, (k, pairs) in enumerate(loads.items())}
        waited = set()

        def ready(k):
            if k not in waited:
                waited.add(k)
                for load in loads[k]:
                    load.wait()

        class Table:
            def __getitem__(self, k):
                ready("early" if k in early else "late")
                return local[k]

        c = Table()
        gx, gy, gz = lax.axis_index("gx"), lax.axis_index("gy"), lax.axis_index("gz")

        def has(dx, dy, dz):
            ok = None
            for g, d, n in ((gx, dx, nx), (gy, dy, ny), (gz, dz, nz)):
                if d:
                    here = (g + d >= 0) if d < 0 else (g + d < n)
                    ok = here if ok is None else ok & here
            return ok

        for k in ("coef", "rhs"):
            loads[k][0].start()
        stages = [0]
        absent = {}

        class Copy:
            def __init__(self, src, dst, there, send_if):
                i = stages[0]
                self.make = lambda: pltpu.make_async_remote_copy(
                    src_ref=src, dst_ref=dst, send_sem=s["ssem"].at[i], recv_sem=s["rsem"].at[i],
                    device_id=there, device_id_type=MESH)
                self.send_if = send_if
                self.hops = 0

            def under(self, f):
                if self.send_if is None:
                    f()
                else:
                    pl.when(self.send_if)(f)

            def start(self):
                self.under(lambda: self.make().start())

            def sent(self):
                self.under(lambda: self.make().wait_send())

        def toward(dx, dy, dz, src, dst, zero):
            i = stages[0]
            absent.setdefault((-dx, -dy, -dz), []).append(lambda: pltpu.make_async_copy(zero, dst, s["rsem"].at[i]).start())
            copy = Copy(src, dst, (gx + dx, gy + dy, gz + dz), has(dx, dy, dz))
            copy.hops = abs(dx) + abs(dy) + abs(dz)
            return copy

        class Stage:
            def __init__(self, make, void, size):
                self.copies = sorted(make(), key=lambda copy: -copy.hops)
                self.i, self.void, self.size = stages[0], void, size
                stages[0] += 1

            def start(self):
                for copy in self.copies:
                    copy.start()

            def drain(self):
                for copy in self.copies:
                    copy.sent()

            def arrive(self):
                all_of_it = self.void.at[0:self.size]
                pltpu.make_async_copy(all_of_it, all_of_it, s["rsem"].at[self.i]).wait()

        def halo0(n):
            fields = 2 if n.start == 0 else 1
            copies = []
            for dx, dy in DIRS:
                if dy == 0:
                    xs = slice(4, 8) if dx > 0 else slice(0, 4)
                    copies.append(toward(dx, dy, 0, s["cells"].at[n, xs], s["x0"].at[n, xs], s["zero16"].at[0:fields]))
                    continue
                face = 0 if dy > 0 else 4
                if dx == 0:
                    mine, to = slice(face, face + 4), slice(face, face + 4)
                else:
                    mine = slice(face + 2, face + 4) if dx > 0 else slice(face, face + 2)
                    first = (8 if dx > 0 else 12) + (0 if dy > 0 else 2)
                    to = slice(first, first + 2)
                copies.append(toward(dx, dy, 0, s["pack0"].at[n, mine], s["y0"].at[n, to], s["zero8"].at[0:fields, 0:to.stop - to.start]))
            return copies

        def slab_halo(slab, slabs, zero, planes=ALL):
            return [toward(dx, dy, dz, slab(0 if dz < 0 else 1, dy), slabs(1 if dz < 0 else 0, ALL.index((-dx, -dy))), zero)
                    for dx, dy in planes for dz in (-1, 1)]

        def plane1(n):
            copies = []
            for dx, dy in DIRS:
                d = ALL.index((-dx, -dy))
                copies.append(toward(dx, dy, 0, s["nat1"].at[n, 0:4], s["nat1"].at[n, 4 * d:4 * d + 4], s["zero8"].at[0]))
            return copies

        def far1(n):
            copies = []
            for dx, dy in FAR:
                e = FAR.index((-dx, -dy))
                i = 3 if dx > 0 else 0
                copies.append(toward(dx, dy, 0, s["nat1"].at[n, i:i + 1], s["nat1"].at[n, 36 + e:37 + e], s["zero8"].at[0, 0:1]))
            return copies

        def z_halo1():
            return [toward(0, 0, -1, s["ext1"].at[8:16, :], s["ext1"].at[R1 - 8:R1, :], s["zero_w"]),
                    toward(0, 0, 1, s["ext1"].at[R1 - 16:R1 - 8, :], s["ext1"].at[0:8, :], s["zero_w"])]

        def yzline():
            mine = s["yz2"].at[0, 1, gy + 4]
            copies = []
            for d in sorted(range(ny), key=lambda d: -min(d, ny - d)):
                for dz in (-1, 1, 0):
                    if d or dz:
                        copies.append(Copy(mine, s["yz2"].at[0, 1 - dz, gy + 4], (gx, lax.rem(gy + d, ny), gz + dz), has(0, 0, dz)))
            i = stages[0]
            for dz in (-1, 1):
                for d in range(ny):
                    absent.setdefault((0, 0, dz), []).append(
                        lambda dz=dz, d=d: pltpu.make_async_copy(s["zero2"], s["yz2"].at[0, 1 + dz, 4 + d], s["rsem"].at[i]).start())
            return copies

        def yzwindow(n, offsets):
            copies = []
            i = stages[0]
            for dy in offsets:
                for dz in (-1, 1, 0):
                    if dy or dz:
                        copy = Copy(s["yz2"].at[n, 1, gy + 4], s["yz2"].at[n, 1 - dz, gy + 4], (gx, gy + dy, gz + dz), has(0, dy, dz))
                        copy.hops = abs(dy) + abs(dz)
                        copies.append(copy)
                        absent.setdefault((0, dy, dz), []).append(
                            lambda dy=dy, dz=dz: pltpu.make_async_copy(s["zero2"], s["yz2"].at[n, 1 + dz, gy + dy + 4], s["rsem"].at[i]).start())
            return copies

        def xline(n, windows):
            copies = []
            for d in sorted(range(1, nx), key=lambda d: -min(d, nx - d)):
                for first, size in windows:
                    at = pl.ds(first, size)
                    copies.append(Copy(s["yz2"].at[n, :, at], s["xs2"].at[n, gx, :, at], (lax.rem(gx + d, nx), gy, gz), None))
            return copies

        E0, E1, C1, Y2, X2, YF, XF = {}, [], [None], [], [], [None], [None]
        for first, fields in ((0, 2), (2, 1)):
            n = slice(first, first + fields)
            E0[first] = Stage(lambda: halo0(n) + slab_halo(lambda side, dy: s["slab0"].at[n, side, 1 if dy else 0],
                                                           lambda side, d: s["slabs0"].at[n, side, d], s["zero8"].at[0:fields, 0]),
                              s["void8"], 50 * fields)
        for n in range(3):
            if n:
                ends = (lambda side, dy: s["slab1"].at[n, side], lambda side, d: s["slabs1"].at[n, side, d], s["zero8"].at[0, 0])
                E1.append(Stage(lambda: slab_halo(*ends, BESIDE) + plane1(n), s["void8"], 42))
                C1.append(Stage(lambda: slab_halo(*ends, CORNERS), s["void8"], 8))
            else:
                E1.append(Stage(lambda: plane1(0) + far1(0), s["void8"], 38))
            if n:
                YF.append(Stage(lambda: yzwindow(n, (-4, -3, 3, 4)), s["void2"], 12))
                Y2.append(Stage(lambda: yzwindow(n, (-2, -1, 0, 1, 2)), s["void2"], 14))
                X2.append(Stage(lambda: xline(n, [(gy + 2, 5)]), s["void2"], (nx - 1) * 15))
                XF.append(Stage(lambda: xline(n, [(gy, 2), (gy + 7, 2)]), s["void2"], (nx - 1) * 12))
            else:
                Y2.append(Stage(yzline, s["void2"], 3 * ny - 1))
                X2.append(Stage(lambda: xline(0, [(4, ny)]), s["void2"], (nx - 1) * 3 * ny))
        Z1 = Stage(z_halo1, s["void8"], 4)

        for k in ("zero16", "zero8", "zero2", "zero_w"):
            s[k][...] = jnp.zeros(s[k].shape, F32)

        barrier = pltpu.get_barrier_semaphore()
        total = jnp.int32(nx - 1 + ny - 1)
        by_distance = sorted(range(ny), key=lambda d: -min(d, ny - d))
        for dz in (-1, 1):
            ok = has(0, 0, dz)
            total = total + ny * ok.astype(jnp.int32)

            @pl.when(ok)
            def _(dz=dz):
                for d in by_distance:
                    pl.semaphore_signal(barrier, inc=1, device_id=(gx, lax.rem(gy + d, ny), gz + dz), device_id_type=MESH)
        for d in by_distance[:-1]:
            pl.semaphore_signal(barrier, inc=1, device_id=(gx, lax.rem(gy + d, ny), gz), device_id_type=MESH)
        for d in range(1, nx):
            pl.semaphore_signal(barrier, inc=1, device_id=(lax.rem(gx + d, nx), gy, gz), device_id_type=MESH)
        near = [(dx, dy, 0) for dx, dy in DIRS + FAR if dx and dy] + [(dx, dy, dz) for dx, dy in DIRS if dx for dz in (-1, 1)]
        for dx, dy, dz in near:
            ok = has(dx, dy, dz)
            total = total + ok.astype(jnp.int32)

            @pl.when(ok)
            def _(dx=dx, dy=dy, dz=dz):
                pl.semaphore_signal(barrier, inc=1, device_id=(gx + dx, gy + dy, gz + dz), device_id_type=MESH)

        for k in ("early", "late"):
            for load in loads[k]:
                load.start()

        for k in ("v0", "v1", "v2"):
            rows = s[k].shape[2]
            for b in range(2):
                for j in range(s[k].shape[1]):
                    s[k][b, j, 0:8] = jnp.zeros((8, 128), F32)
                    s[k][b, j, rows - 8:rows] = jnp.zeros((8, 128), F32)
        s["nat1"][0, 42:48] = jnp.zeros((6, 8, 128), F32)
        for n in (1, 2):
            s["nat1"][n, 36:48] = jnp.zeros((12, 8, 128), F32)

        def post0(n, nat, flipped):
            cells = nat.reshape(8, 16, 128)
            high, low = cells[:, 12:16].reshape(32, 128), cells[:, 0:4].reshape(32, 128)
            s["pack0"][n, 0:4] = high.reshape(4, 8, 128)
            s["pack0"][n, 4:8] = low.reshape(4, 8, 128)
            faces = jnp.concatenate([high, low, high[16:32], low[16:32], high[0:16], low[0:16]], axis=0).T
            for kind, rows in enumerate((flipped, faces)):
                s["slab0"][n, 0, kind] = rows[0:8]
                s["slab0"][n, 1, kind] = rows[120:128]

        lane = lax.broadcasted_iota(jnp.int32, (8, 128), 1)

        def by_quarter(parts):
            return jnp.where(lane < 32, parts[0], jnp.where(lane < 64, parts[1], jnp.where(lane < 96, parts[2], parts[3])))

        ready("coef")
        k_nat = coef[...].reshape(128, 128)
        k_flip = k_nat.T
        post0(1, k_nat, k_flip)
        ready("rhs")
        f_nat = rhs[...].reshape(128, 128)
        f_flip = f_nat.T
        post0(0, f_nat, f_flip)
        pl.semaphore_wait(barrier, total)
        E0[0].start()
        for place, fills in absent.items():
            @pl.when(jnp.logical_not(has(*place)))
            def _(fills=fills):
                for fill in fills:
                    fill()

        k1 = times(left(c["kx1"][...], k_nat), c["kz1"][...])
        s["nat1"][0, 0:4] = k1.reshape(4, 8, 128)
        E1[0].start()
        k2_parts = times(left(c["kx2"][...], k_nat), c["kz2"][...])
        s["yz2"][0, 1, gy + 4] = by_quarter([k2_parts[8 * q:8 * q + 8] for q in range(4)])[0:2]
        Y2[0].start()

        def shifts(v, xe):
            rows, lanes = v.shape
            tiles = [v[:, i:i + 128] for i in range(0, lanes, 128)]
            if 128 % xe or len(tiles) == 1:
                beside = (pltpu.roll(v, lanes - 1, 1), pltpu.roll(v, 1, 1))
            else:
                beside = tuple(jnp.concatenate([pltpu.roll(tile, d, 1) for tile in tiles], axis=1) for d in (127, 1))
            return beside + (pltpu.roll(v, lanes - xe, 1), pltpu.roll(v, xe, 1),
                    pltpu.roll(v, rows - 1, 0), pltpu.roll(v, 1, 0))

        def setup(k, xe, factor, inside, inner, extra, m, consts_ref):
            rows, lanes = k.shape
            ws = []
            for i, other in enumerate(shifts(k, xe)):
                if inner is not None and i < 4:
                    other = jnp.where(inner[i], other, 0.0)
                ws.append(0.5 * (k + other))
            diag = ws[0]
            for w in ws[1:]:
                diag = diag + w
            diag = factor * diag
            minv = jnp.where(inside, 0.8 / diag, 0.0)
            for i, w in enumerate(ws):
                link = (factor * minv) * w
                if inner is not None and i < 4:
                    link = jnp.where(inner[i], link, 0.0)
                if extra is not None:
                    link = jnp.where(extra[i], link, 0.0)
                m[i] = link
            consts_ref[0] = minv
            if consts_ref.shape[0] > 2:
                consts_ref[1] = 1.25 * diag

        def sweep(v, g, m, xe, first=0):
            total = 0.2 * v + g
            for i, other in enumerate(shifts(v, xe)):
                total = total + m[i, first:first + v.shape[0]] * other
            return total

        def put(vs, k, value, first=0):
            for j in range(vs.shape[1]):
                vs[k, j, 8 + first:8 + first + value.shape[0]] = value[:, 128 * j:128 * j + 128]

        def get(vs, k, rows, first=0):
            parts = [vs[k, j, 8 + first:8 + first + rows] for j in range(vs.shape[1])]
            return parts[0] if len(parts) == 1 else jnp.concatenate(parts, axis=1)

        def sweep_in(vs, a, b, g, m, xe, rows, first=0):
            count = vs.shape[1]

            def body(i, carry):
                row = first + 8 * i
                at = pl.ds(pl.multiple_of(row, 8), 8)
                centre = [vs[a, j, pl.ds(row + 8, 8), :] for j in range(count)]
                right, left_, above, below = ([pltpu.roll(v, d, 1) for v in centre] for d in (127, 1, 128 - xe, xe))
                for j in range(count):
                    after, before = (j + 1) % count, (j - 1) % count
                    lanes = slice(128 * j, 128 * j + 128)
                    xr, xl, yr, yl = right[j], left_[j], above[j], below[j]
                    if count > 1:
                        if 128 % xe:
                            xr = jnp.where(lane < 127, xr, right[after])
                            xl = jnp.where(lane > 0, xl, left_[before])
                        yr = jnp.where(lane < 128 - xe, yr, above[after])
                        yl = jnp.where(lane >= xe, yl, below[before])
                    total = 0.2 * centre[j] + g[at, lanes]
                    others = (xr, xl, yr, yl, vs[a, j, pl.ds(row + 9, 8), :], vs[a, j, pl.ds(row + 7, 8), :])
                    for q, other in enumerate(others):
                        total = total + m[q, at, lanes] * other
                    vs[b, j, pl.ds(row + 8, 8), :] = total
                return carry

            lax.fori_loop(0, rows // 8, body, 0, unroll=True)

        def coords(level, lanes, rows, x_off, y_off, z_off):
            x = c["coord"][2 * level:2 * level + 1, 0:lanes] + x_off
            y = c["coord"][2 * level + 1:2 * level + 2, 0:lanes] + y_off
            z = lax.broadcasted_iota(jnp.int32, (rows, lanes), 0) + z_off
            return x, y, z

        def inside_of(x, y, z, sizes):
            plane = (x >= 0) & (x < sizes[0]) & (y >= 0) & (y < sizes[1])
            return jnp.broadcast_to(plane, z.shape) & (z >= 0) & (z < sizes[2])

        def assemble0(n, flipped):
            blocks = [flipped, s["x0"][n].reshape(128, 128).T, s["y0"][n].reshape(128, 128).T]
            ends = []
            for side in range(2):
                def at(dx, dy, side=side):
                    return s["slabs0"][n, side, ALL.index((dx, dy))]

                diagonals = jnp.where(lane < 80, at(-1, -1), jnp.where(lane < 96, at(-1, 1), jnp.where(lane < 112, at(1, -1), at(1, 1))))
                ends.append(jnp.concatenate([
                    at(0, 0), jnp.where(lane < 64, at(1, 0), at(-1, 0)),
                    jnp.where(lane < 32, at(0, -1), jnp.where(lane < 64, at(0, 1), diagonals))], axis=1))
            wide = jnp.concatenate([ends[0], jnp.concatenate(blocks, axis=1), ends[1]], axis=0)
            return times(wide, c["place0"][...])

        def natural1(n):
            nat = s["nat1"][n].reshape(384, 128)
            return jnp.concatenate([nat[128 * i:128 * i + 128].T for i in range(3)], axis=1)[0:64]

        def slabs_of(n, side, planes):
            slabs = [s["slabs1"][n, side, d] if ALL[d] in planes else jnp.zeros((8, 128), F32) for d in range(9)]
            return jnp.concatenate([by_quarter(slabs[0:4]), by_quarter(slabs[4:8]), jnp.where(lane < 32, slabs[8], 0.0)], axis=1)

        def assemble1(n):
            ends = [slabs_of(n, side, BESIDE) for side in range(2)]
            wide = jnp.concatenate([ends[0], natural1(n), ends[1]], axis=0)
            return times(wide, c["place1"][...])

        def corners1(n):
            C1[n].arrive()
            more = times(jnp.concatenate([slabs_of(n, side, CORNERS) for side in range(2)], axis=0), c["place1"][...])
            for rows, part in ((slice(0, 8), more[0:8]), (slice(R1 - 8, R1), more[8:16])):
                s["c1"][2, rows] = s["c1"][2, rows] + s["c1"][0, rows] * part
            presmooth(s["v1"], s["m1"], s["c1"], XE1)

        def drain(*done):
            for stage in done:
                stage.drain()

        def gather2_x(n):
            Y2[n].arrive()
            X2[n].start()
            if n:
                YF[n].arrive()
                XF[n].start()
            s["xs2"][n, gx] = s["yz2"][n]

        def gather2(n):
            X2[n].arrive()
            if n:
                XF[n].arrive()
            rows = []
            for dz in range(3):
                flipped = s["xs2"][n, :, dz, 4:4 + ny].reshape(nx * ny * 2, 128).T
                rows.append(jnp.concatenate([flipped[32 * q:32 * q + 32] for q in range(4)], axis=1))
            wide = jnp.concatenate(rows, axis=0)
            if n:
                device = c["coord"][14:15, 0:wide.shape[1]] - gy
                wide = jnp.where((device >= -4) & (device <= 4), wide, 0.0)
            return times(wide, c["perm2"][...])

        x1, y1, z1 = coords(1, L1, R1, 4 * gx, 8 * gy, 64 * gz - 8)
        target = c["coord"][8:9, 0:L1] + (2 * gx + 4 * gy * x2)
        target = jnp.where((x1 >= 0) & (x1 < 4 * nx) & (y1 >= 0) & (y1 < 8 * ny), target, -1)
        s["prol1"][...] = jnp.where(lax.broadcasted_iota(jnp.int32, (l2, L1), 0) == target, 1.0, 0.0).astype(BF16)

        near_owner = []
        xb = c["coord"][6:7, 0:l3]
        for i in (jnp.maximum(gz - 1, 0), gz, jnp.minimum(gz + 1, nz - 1)):
            pick = lax.broadcasted_iota(jnp.int32, (2 * ny * nz, l3), 0) == c["coord"][9:10, 0:l3] + i
            picked = jnp.dot(s["agg"][...].astype(F32).astype(BF16), jnp.where(pick, 1.0, 0.0).astype(BF16), preferred_element_type=F32)
            mine = jnp.zeros((1, l3), F32)
            for r in range(nx // 2):
                mine = jnp.where(xb // 2 == r, picked[r:r + 1], mine)
            near_owner.append(jnp.broadcast_to(mine, (16, l3)))
        owner = jnp.concatenate(near_owner, axis=0)

        E0[0].arrive()
        k0 = assemble0(1, k_flip)
        x0, y0, z0 = coords(0, L0, R0, 8 * gx, 16 * gy, 128 * gz - 8)
        setup(k0, XE0, 1.0, inside_of(x0, y0, z0, (8 * nx, 16 * ny, 128 * nz)), None, None, s["m0"], s["c0"])
        f0 = assemble0(0, f_flip)
        s["rhs0"][...] = f0
        s["c0"][2] = s["c0"][0] * f0

        def halved(v, first, half):
            rows, lanes = v.shape
            sums = []
            for j in range(lanes // 128):
                s["pairs"][j, 0:rows] = v[:, 128 * j:128 * j + 128]
                sums.append(s["pairs"][j, pl.ds(first, half, stride=2), :] + s["pairs"][j, pl.ds(first + 1, half, stride=2), :])
            return sums[0] if len(sums) == 1 else jnp.concatenate(sums, axis=1)

        def doubled(v, first, rows):
            half, lanes = v.shape
            parts = []
            for j in range(lanes // 128):
                part = v[:, 128 * j:128 * j + 128]
                s["pairs"][j, pl.ds(0, half, stride=2), :] = part
                s["pairs"][j, pl.ds(1, half, stride=2), :] = part
                parts.append(s["pairs"][j, first:first + rows])
            return parts[0] if len(parts) == 1 else jnp.concatenate(parts, axis=1)

        def presmooth(vs, m, consts_ref, xe):
            put(vs, 0, consts_ref[2])
            sweep_in(vs, 0, 1, consts_ref.at[2], m, xe, m.shape[1])

        def down(vs, m, consts_ref, xe):
            rows = m.shape[1]
            presmooth(vs, m, consts_ref, xe)
            sweep_in(vs, 1, 0, consts_ref.at[2], m, xe, rows)
            return consts_ref[1] * (get(vs, 0, rows) - get(vs, 1, rows))

        def up(vs, m, consts_ref, xe, correction, first=0):
            rows = correction.shape[0]
            put(vs, 0, get(vs, 1, rows, first) + correction, first)
            sweep_in(vs, 0, 1, consts_ref.at[2], m, xe, rows, first)
            sweep_in(vs, 1, 0, consts_ref.at[2], m, xe, rows, first)
            return get(vs, 0, rows, first)

        E1[0].arrive()
        s["ext1"][8:R1 - 8] = times(natural1(0), c["place1"][...])
        Z1.start()

        for cycle in range(2):
            n = 1 + cycle
            r = down(s["v0"], s["m0"], s["c0"], XE0)
            half = halved(r, 8, 64)
            ends = times(jnp.concatenate([half[0:8], half[56:64]], axis=0), c["sel0r"][...])
            s["slab1"][n] = ends.reshape(2, 8, 128)
            s["nat1"][n, 0:4, :, 0:64] = select_t(c["sel0"][...], half).reshape(4, 8, 64)
            E1[n].start()
            C1[n].start()
            if cycle == 0:
                gather2_x(0)
                Z1.arrive()
                inside = inside_of(x1, y1, z1, (4 * nx, 8 * ny, 64 * nz))
                setup(s["ext1"][...], XE1, 0.25, inside, None, None, s["m1"], s["c1"])
            if cycle == 1:
                drain(X2[1], XF[1])
            E1[n].arrive()
            s["c1"][2] = s["c1"][0] * assemble1(n)
            half = halved(down(s["v1"], s["m1"], s["c1"], XE1), 8, 32)
            quarters = [jnp.where(c["coord"][10 + q:11 + q, 0:L1] > 0, half, 0.0) for q in range(4)]
            s["yz2"][n, 1, gy + 4] = select_t(c["sel1"][...], jnp.concatenate(quarters, axis=0))[0:2]
            YF[n].start()
            Y2[n].start()
            if cycle == 0:
                k2 = gather2(0)
                x, y, z = coords(2, l2, R2, 0, 0, 32 * gz - 32)
                inner = [jnp.broadcast_to(q, z.shape) for q in (x + 1 < x2, x > 0, y + 1 < y2, y > 0)]
                setup(k2, x2, 0.0625, inside_of(x, y, z, (x2, y2, 32 * nz)), inner, None, s["m2"], s["c2"])
                k3 = times(halved(k2, 0, R3), c["rest2"][...])
                x, y, z = coords(3, l3, R3, 0, 0, 16 * gz - 16)
                inner = [jnp.broadcast_to(q, z.shape) for q in (x + 1 < nx, x > 0, y + 1 < 2 * ny, y > 0)]
                same = [other == owner for other in shifts(owner, nx)]
                setup(k3, nx, 0.015625, inside_of(x, y, z, (nx, 2 * ny, 16 * nz)), inner, same, s["m3"], s["c3"])
            if cycle == 0:
                drain(E0[0], E1[0], Y2[0], Z1)
            else:
                drain(E0[2])
            corners1(n)
            gather2_x(n)
            if cycle == 0:
                drain(E1[1], C1[1], X2[0])
            else:
                drain(E1[2], C1[2], Y2[2], YF[2])
            f2 = gather2(n)
            s["c2"][2] = s["c2"][0] * f2
            r = down(s["v2"], s["m2"], s["c2"], x2)
            g3 = s["c3"][0] * times(halved(r, 0, R3), c["rest2"][...])
            e = g3
            for j in range(COARSE_SWEEPS - 1):
                e = sweep(e, g3, s["m3"], nx)
            v = up(s["v2"], s["m2"], s["c2"], x2, doubled(times(e[8:40], c["prol2"][...]), 8, 48), 24)
            fine = times(v, s["prol1"][...])
            v = up(s["v1"], s["m1"], s["c1"], XE1, doubled(fine, 8, R1))
            fine = times(v, c["prol0"][...])
            v = up(s["v0"], s["m0"], s["c0"], XE0, doubled(fine, 8, R0))
            nat = select_t(c["unsel"][...], v[8:R0 - 8])
            if cycle == 0:
                s["cells"][2] = nat.reshape(8, 16, 128)
                flipped = nat.T
                post0(2, nat, flipped)
                E0[2].start()
                drain(Y2[1], YF[1])
                E0[2].arrive()
                now = assemble0(2, flipped)
                put(s["v0"], 0, now)
                s["c0"][2] = s["c0"][0] * s["rhs0"][...]
                sweep_in(s["v0"], 0, 1, s["c0"].at[2], s["m0"], XE0, R0)
                s["c0"][2] = get(s["v0"], 1, R0) - get(s["v0"], 0, R0)
            else:
                out[...] = s["cells"][2] + nat.reshape(8, 16, 128)
        for k in loads:
            ready(k)
        drain(X2[2], XF[2])

    vmem = pl.BlockSpec(memory_space=pltpu.VMEM)
    hbm = pl.BlockSpec(memory_space=pl.ANY)

    def body(rhs, coef, agglom):
        agg = agglom.reshape(nx // 2, 2 * ny * nz)
        return pl.pallas_call(
            kernel,
            out_shape=pltpu.VMEM((8, 16, 128), F32),
            in_specs=[hbm, hbm, hbm] + [hbm] * len(names),
            out_specs=vmem,
            scratch_shapes=[scratch[k] for k in keys] + held,
            compiler_params=pltpu.CompilerParams(collective_id=0, has_side_effects=True, vmem_limit_bytes=60 * 1024 * 1024),
        )(rhs, coef, agg, *[jnp.asarray(consts[k]) for k in names])

    return body


def solution(mesh):
    body = build(mesh.shape["gx"], mesh.shape["gy"], mesh.shape["gz"])
    spec = P("gx", "gy", "gz")
    return jax.shard_map(body, mesh=mesh, in_specs=(spec, spec, P()), out_specs=spec, check_vma=False)
```
